32 devices in a mesh: shift: 2 (over y), row: 8 (over z, x), col: 2 (over core).
Axes of the slice: x: 2, y: 2, z: 4, core: 2. Of those that a mesh axis runs over, the one named last changes fastest.
Arguments:
- krylov_basis: float32 [128, 3, 8, 8, 128], P('shift', None, 'row', 'col'), parts along dimension 0, may hold values from -4000 to 4000, as said below
- regions: int32 [8, 8, 128], P('row', 'col'), may hold values from 0 to 7
- mu_table: float32 [8], replicated, may hold values from 0.5 to 2
- eps_table: float32 [8], replicated, may hold values from 1 to 4
- shift_value: float32 [2], P('shift'), parts along dimension 0, may hold values from 0.5 to 2
Outputs:
- orthonormal: float32 [128, 3, 8, 8, 128], P('shift', None, 'row', 'col'), parts along dimension 0
- upper_factor: float32 [128, 64], P('shift'), parts along dimension 0
- applied: float32 [128, 3, 8, 8, 128], P('shift', None, 'row', 'col'), parts along dimension 0
- projected: float32 [128, 64], P('shift'), parts along dimension 0
The draws below stay inside these ranges and needn't reach their ends.
There are 2 independent parts, one for each index of `shift`. The reference program is written for one: setup_inputs(seed, part) draws one part's arguments, and reference() takes and returns one part's arrays. A program takes and returns all parts, laid end to end along the dimension named above; an argument that names none is the same for every part. Nothing has to cross between parts.
Inputs may be any that keep to these rules, and one draw needn't show every extreme that they name: `krylov_basis`: Real-valued entries.
All inputs are finite; a program needn't handle non-finite values.
Results may differ from the reference program's by a relative error of at most 0.000071.
Values sent between devices are 32-bit elements; how exact they have to be, the bound alone decides.
A program may use at most 64 MiB of HBM per device.

```python
import math
import jax
import jax.numpy as jnp
from jax import lax

COLS = 64
NZ = 128
NREG = 8
NX = 8
NY = 8


def draw_krylov_basis(key, part):
    keys = jax.random.split(jax.random.fold_in(key, 71), 3)
    normals = jnp.clip(jax.random.normal(keys[0], (COLS, 3, NX, NY, NZ), jnp.float32), -5.0, 5.0)
    position = jnp.arange(NX, dtype=jnp.float32) / max(NX - 1, 1)
    along_x = 1.0 + 2.0 * position
    column_scale = jnp.exp(jax.random.uniform(keys[1], (COLS,), jnp.float32) * jnp.log(10.0))
    cell_scale = jnp.exp(jax.random.uniform(keys[2], (3, NX, NY, NZ), jnp.float32) * jnp.log(3.0))
    scaled = normals * column_scale[:, None, None, None, None]
    scaled = scaled * along_x[None, None, :, None, None] * cell_scale[None]
    return scaled.astype(jnp.float32)


def set_ends(entries, stream_key, low, high):
    longest = entries.shape.index(max(entries.shape))
    spots = []
    for shift in (0, 1):
        where = [jax.random.randint(jax.random.fold_in(stream_key, axis), (), 0, length) for axis, length in enumerate(entries.shape)]
        where[longest] = (where[longest] + shift) % entries.shape[longest]
        spots.append(tuple(where))
    return entries.at[spots[0]].set(low).at[spots[1]].set(high)


def setup_inputs(seed: int = 0, part: int = 0) -> dict:
    streams_of = jax.random.split(jax.random.key(seed), 6)
    part_keys = jax.random.split(jax.random.fold_in(streams_of[5], part), 6)
    return {
        "krylov_basis": draw_krylov_basis(jax.random.fold_in(jax.random.fold_in(streams_of[5], part), 71), part),
        "regions": set_ends(jax.random.randint(streams_of[1], (NX, NY, NZ), 0, NREG), jax.random.fold_in(streams_of[1], 1), 0, NREG - 1).astype(jnp.int32),
        "mu_table": jnp.clip(jnp.exp(jax.random.uniform(streams_of[2], (NREG,), jnp.float32, math.log(0.5), math.log(2.0))), 0.5, 2.0),
        "eps_table": jnp.clip(jnp.exp(jax.random.uniform(streams_of[3], (NREG,), jnp.float32, math.log(1.0), math.log(4.0))), 1.0, 4.0),
        "shift_value": jnp.clip(jax.random.uniform(part_keys[4], (1,), jnp.float32, 0.5, 2.0), 0.5, 2.0),
    }


def forward_z(values):
    return jnp.pad(values[..., 1:], ((0, 0), (0, 0), (0, 0), (0, 1))) - values

def backward_z(values):
    return values - jnp.pad(values[..., :-1], ((0, 0), (0, 0), (0, 0), (1, 0)))

def operator_block(padded_field, coupling, permittivity, shift_scalar):
    cells_x = padded_field.shape[2] - 2
    cells_y = padded_field.shape[3] - 2
    field_x = padded_field[:, 0]
    field_y = padded_field[:, 1]
    field_z = padded_field[:, 2]

    def corner_part(values):
        return values[:, :cells_x + 1, :cells_y + 1]

    def forward_x(values):
        return values[:, 1:cells_x + 2, :cells_y + 1] - corner_part(values)

    def forward_y(values):
        return values[:, :cells_x + 1, 1:cells_y + 2] - corner_part(values)

    def forward_dz(values):
        return forward_z(corner_part(values))
    curl_x = forward_y(field_z) - forward_dz(field_y)
    curl_y = forward_dz(field_x) - forward_x(field_z)
    curl_z = forward_x(field_y) - forward_y(field_x)
    weighted_x = coupling * curl_x
    weighted_y = coupling * curl_y
    weighted_z = coupling * curl_z

    def backward_x(values):
        return values[:, 1:, 1:] - values[:, :-1, 1:]

    def backward_y(values):
        return values[:, 1:, 1:] - values[:, 1:, :-1]

    def backward_dz(values):
        return backward_z(values[:, 1:, 1:])
    result_x = backward_y(weighted_z) - backward_dz(weighted_y)
    result_y = backward_dz(weighted_x) - backward_x(weighted_z)
    result_z = backward_x(weighted_y) - backward_y(weighted_x)
    interior = padded_field[:, :, 1:cells_x + 1, 1:cells_y + 1]
    stacked = jnp.stack([result_x, result_y, result_z], axis=1)
    return stacked - shift_scalar * permittivity * interior

def reference(krylov_basis, regions, mu_table, eps_table, shift_value):
    total_rows = 3 * NX * NY * NZ
    flattened = krylov_basis.reshape(COLS, -1)
    gram_matrix = jnp.dot(flattened.astype(jnp.float32), flattened.T.astype(jnp.float32), precision=lax.Precision.HIGHEST, preferred_element_type=jnp.float32) / total_rows
    lower_factor = jnp.linalg.cholesky(gram_matrix)
    upper_factor = lower_factor.T
    inverse = lax.linalg.triangular_solve(lower_factor, jnp.eye(COLS, dtype=jnp.float32), left_side=True, lower=True)
    ortho_flat = jnp.dot(inverse.astype(jnp.float32), flattened.astype(jnp.float32), precision=lax.Precision.HIGHEST, preferred_element_type=jnp.float32)
    orthonormal = ortho_flat.reshape(krylov_basis.shape)
    coupling = jnp.pad(mu_table[regions], ((1, 0), (1, 0), (0, 0)))
    permittivity = eps_table[regions]
    shift_scalar = shift_value[0]
    blocks = orthonormal.reshape((COLS // 8, 8) + krylov_basis.shape[1:])

    def apply_block(column_block):
        padded_field = jnp.pad(column_block, ((0, 0), (0, 0), (1, 1), (1, 1), (0, 0)))
        return operator_block(padded_field, coupling, permittivity, shift_scalar)
    applied = lax.map(apply_block, blocks).reshape(krylov_basis.shape)
    projected = jnp.dot(ortho_flat.astype(jnp.float32), applied.reshape(COLS, -1).T.astype(jnp.float32), precision=lax.Precision.HIGHEST, preferred_element_type=jnp.float32) / total_rows
    return (orthonormal, upper_factor, applied, projected)
```

```python
import functools

import jax
import jax.numpy as jnp
from jax import lax
from jax.experimental import pallas as pl
from jax.experimental.pallas import tpu as pltpu
from jax.sharding import PartitionSpec as P

F32 = jnp.float32
BF16 = jnp.bfloat16
MESH = pl.DeviceIdType.MESH
COL, MCOPY, DOWN, UP = 0, 1, 2, 6
REDUCE = 10
PAIR_OUT, PAIR_IN, NEAR_OUT, NEAR_IN, FAR_OUT, FAR_IN, HALF, OTHER, MORE = 0, 1, 2, 3, 4, 5, 8, 9, 10


def split3(x):
    high = x.astype(BF16)
    rest = x - high.astype(F32)
    mid = rest.astype(BF16)
    low = (rest - mid.astype(F32)).astype(BF16)
    return high, mid, low


def rows_dot(a, b):
    return lax.dot_general(a, b, (((1,), (1,)), ((), ())), preferred_element_type=F32)


def plain_dot(a, b):
    return lax.dot_general(a, b, (((1,), (0,)), ((), ())), preferred_element_type=F32)


def first_dot(a, b):
    return lax.dot_general(a, b, (((0,), (0,)), ((), ())), preferred_element_type=F32)


def inner(left, right=None):
    n = left.shape[0]
    a, b, c = split3(left)
    d, e, f = (a, b, c) if right is None else split3(right)
    first = rows_dot(jnp.concatenate([a, b, c], axis=0), d)
    second = rows_dot(jnp.concatenate([a, b], axis=0), e)
    third = rows_dot(a, f)
    return first[:n] + ((first[n : 2 * n] + second[:n]) + ((first[2 * n :] + third) + second[n:]))


def times(left, right):
    a, b, c = split3(left)
    d, e, f = split3(right)
    return plain_dot(
        jnp.concatenate([a, a, b, b, a, c], axis=1), jnp.concatenate([d, e, d, e, f, d], axis=0)
    )


def factor(gram):
    n = gram.shape[0]
    size = 16
    wide = 2 * n
    rows_of = lax.broadcasted_iota(jnp.int32, (n, n), 0)
    eye = (rows_of == lax.broadcasted_iota(jnp.int32, (n, n), 1)).astype(F32)
    rest = jnp.concatenate([gram, eye], axis=1)
    place = lax.broadcasted_iota(jnp.int32, (size, wide), 0)
    done, pivots = [], []
    for block in range(n // size):
        rows = rest[:size]
        begin = block * size
        cols = [
            jnp.broadcast_to(rows[:, begin + j : begin + j + 1], (size, wide)) for j in range(size)
        ]
        pivot = jnp.zeros((size, wide), F32)
        inverse = jnp.zeros((size, wide), F32)
        for k in range(size):
            head = jnp.broadcast_to(cols[k][k : k + 1], (size, wide))
            reciprocal = 1.0 / head
            pivot = jnp.where(place == k, head, pivot)
            inverse = jnp.where(place == k, reciprocal, inverse)
            if k < size - 1:
                ratio = jnp.where(place > k, cols[k] * reciprocal, 0.0)
                for j in range(k + 1, size):
                    cols[j] = cols[j] - ratio * jnp.broadcast_to(cols[j][k : k + 1], (size, wide))
                rows = rows - ratio * jnp.broadcast_to(rows[k : k + 1], (size, wide))
        done.append(rows)
        pivots.append(pivot)
        if begin + size < n:
            a, b, c = split3((rows * inverse)[:, :n])
            d, e, f = split3(rows)
            update = first_dot(
                jnp.concatenate([a, a, b, b, a, c], axis=0),
                jnp.concatenate([d, e, d, e, f, d], axis=0),
            )
            rest = rest[size:] - update[begin + size :]
    pivot = jnp.concatenate(pivots, axis=0)
    scaled = jnp.concatenate(done, axis=0) / jnp.sqrt(pivot)
    keep = lax.broadcasted_iota(jnp.int32, (n, wide), 1) >= lax.broadcasted_iota(
        jnp.int32, (n, wide), 0
    )
    return jnp.where(keep, scaled, 0.0)


def select(condition, a, b):
    return jnp.where(condition, a, b)


def main_kernel(
    peers,
    total,
    x_ref,
    regions_ref,
    mu_ref,
    eps_ref,
    shift_ref,
    tiles_ref,
    image_ref,
    wide_ref,
    proj_ref,
    landed,
    below,
    beside,
    edge,
    edge_out,
    up_out,
    up_in,
    sums,
    load_sem,
    send_sem,
    recv_sem,
):
    r = lax.axis_index("row")
    c = lax.axis_index("col")
    n = landed.shape[0] // 12
    first, last = r == 0, r == peers - 1
    bits = peers.bit_length() - 1
    far = [m for m in (2, 4, 6) if m < peers]
    more = [1 << b for b in range(3, bits)]

    load = pltpu.make_async_copy(x_ref, landed, load_sem)
    load.start()

    def other(mask):
        return {"row": jnp.bitwise_xor(r, mask)}

    sibling = {"col": 1 - c}
    barrier = pltpu.get_barrier_semaphore()
    pl.semaphore_signal(barrier, inc=1, device_id=sibling, device_id_type=MESH)
    for mask in far + more:
        pl.semaphore_signal(barrier, inc=1, device_id=other(mask), device_id_type=MESH)

    @pl.when(r > 0)
    def _():
        pl.semaphore_signal(barrier, inc=1, device_id={"row": r - 1}, device_id_type=MESH)

    @pl.when(r < peers - 1)
    def _():
        pl.semaphore_signal(barrier, inc=1, device_id={"row": r + 1}, device_id_type=MESH)

    labels = regions_ref[0]
    mu = jnp.zeros(labels.shape, F32)
    eps = jnp.zeros(labels.shape, F32)
    for region in range(mu_ref.shape[0]):
        mu = jnp.where(labels == region, mu_ref[region], mu)
        eps = jnp.where(labels == region, eps_ref[region], eps)
    eps = eps * shift_ref[0]

    def over(row):
        return jnp.broadcast_to(row, (n, 128))

    mu_y = [over(mu[y : y + 1]) for y in range(4)]
    eps_y = [over(eps[y : y + 1]) for y in range(4)]

    load.wait()
    for y in range(4):
        for comp in range(3):
            tiles_ref[3 * y + comp] = landed[pl.ds(comp * 4 + y, n, stride=12), :]

    def remote(index, source, target, device):
        return pltpu.make_async_remote_copy(
            src_ref=source,
            dst_ref=target,
            send_sem=send_sem.at[index],
            recv_sem=recv_sem.at[index],
            device_id=device,
            device_id_type=MESH,
        )

    beside_copy = remote(COL, tiles_ref.at[pl.ds(0, 3)], beside, sibling)
    edge_copy = remote(MCOPY, edge_out, edge, sibling)
    lower = {"row": jnp.maximum(r - 1, 0)}
    upper = {"row": jnp.minimum(r + 1, peers - 1)}
    down = [
        remote(DOWN + y, tiles_ref.at[pl.ds(3 * y + 1, 2)], below.at[pl.ds(2 * y, 2)], lower)
        for y in range(4)
    ]
    up = [remote(UP + y, up_out.at[y], up_in.at[y], upper) for y in range(4)]

    @pl.when(last)
    def _():
        below[...] = jnp.zeros_like(below)

    @pl.when(first)
    def _():
        up_in[...] = jnp.zeros_like(up_in)

    @pl.when(c == 1)
    def _():
        beside[...] = jnp.zeros_like(beside)

    @pl.when(c == 0)
    def _():
        edge[...] = jnp.zeros_like(edge)

    pl.semaphore_wait(
        barrier, 1 + len(far) + len(more) + jnp.where(first, 0, 1) + jnp.where(last, 0, 1)
    )

    @pl.when(c == 1)
    def _():
        beside_copy.start()

    @pl.when(r > 0)
    def _():
        for copy in down:
            copy.start()

    def reduction(which):
        base = REDUCE + which * (6 + len(more))
        slot = sums.at[which]
        pair = remote(base, slot.at[PAIR_OUT], slot.at[PAIR_IN], sibling)
        near = remote(base + 1, slot.at[NEAR_OUT], slot.at[NEAR_IN], other(1))
        fars = [
            remote(base + 2 + i, slot.at[FAR_OUT], slot.at[FAR_IN + i], other(mask))
            for i, mask in enumerate(far)
        ]
        back = remote(base + 5, slot.at[HALF], slot.at[OTHER], sibling)
        further = [
            remote(base + 6 + i, slot.at[MORE + 2 * i], slot.at[MORE + 2 * i + 1], other(mask))
            for i, mask in enumerate(more)
        ]
        used = [pair] + ([near] if peers > 1 else []) + fars + [back] + further

        def begin(value):
            packed = jnp.concatenate([value[: n // 2], value[n // 2 :]], axis=1)
            q = n // 4
            slot[PAIR_OUT] = jnp.where(c == 0, packed[q:], packed[:q])
            slot[NEAR_OUT] = jnp.where(c == 0, packed[:q], packed[q:])
            pair.start()

        def step_near():
            pair.wait_recv()
            slot[NEAR_OUT] = slot[NEAR_OUT] + slot[PAIR_IN]
            near.start()

        def step_far():
            near.wait_recv()
            slot[FAR_OUT] = slot[NEAR_OUT] + slot[NEAR_IN]
            for copy in fars:
                copy.start()

        def step_back():
            got = slot[FAR_OUT]
            for i, copy in enumerate(fars):
                copy.wait_recv()
                got = got + slot[FAR_IN + i]
            for i, copy in enumerate(further):
                slot[MORE + 2 * i] = got
                copy.start()
                copy.wait_recv()
                got = got + slot[MORE + 2 * i + 1]
            slot[HALF] = got
            back.start()

        def end():
            back.wait_recv()
            mine, theirs = slot[HALF], slot[OTHER]
            packed = jnp.concatenate(
                [jnp.where(c == 0, mine, theirs), jnp.where(c == 0, theirs, mine)], axis=0
            )
            return jnp.concatenate([packed[:, :n], packed[:, n:]], axis=0) * (1.0 / total)

        return begin, step_near, step_far, step_back, end, used

    gram_begin, gram_near, gram_far, gram_back, gram_end, gram_used = reduction(0)
    proj_begin, proj_near, proj_far, proj_back, proj_end, proj_used = reduction(1)

    every = jnp.concatenate([tiles_ref[t] for t in range(12)], axis=1)
    gram_begin(inner(every))

    lane = lax.broadcasted_iota(jnp.int32, (n, 128), 1)

    def forward(values):
        return jnp.where(lane == 127, 0.0, pltpu.roll(values, 127, 1)) - values

    def backward(values):
        return values - jnp.where(lane == 0, 0.0, pltpu.roll(values, 1, 1))

    def ex(y):
        return tiles_ref[3 * y] if y < 4 else beside[0]

    def ey(y):
        return tiles_ref[3 * y + 1]

    def ez(y):
        return tiles_ref[3 * y + 2] if y < 4 else beside[2]

    def combine(y):
        up_out[y, pl.ds(0, n)] = ey(y) + (ex(y + 1) - ex(y))
        up_out[y, pl.ds(n, n)] = ez(y) + forward(ex(y))
        up_out[y, pl.ds(2 * n, 8)] = jnp.broadcast_to(mu[y : y + 1], (8, 128))

    for y in range(3):
        combine(y)

    gram_near()

    @pl.when(c == 0)
    def _():
        beside_copy.wait_recv()

    combine(3)

    @pl.when(r < peers - 1)
    def _():
        for copy in up:
            copy.start()

    curl_x = [ez(y + 1) - ez(y) - forward(ey(y)) for y in range(4)]
    m_x = [mu_y[y] * curl_x[y] for y in range(4)]
    left = jnp.concatenate(
        m_x + [-eps_y[y] * tiles_ref[3 * y + comp] for y in range(4) for comp in range(3)], axis=1
    )
    right = jnp.concatenate(curl_x + [tiles_ref[t] for y in range(4) for t in range(3 * y, 3 * y + 3)], axis=1)
    partial = inner(left, right)
    edge_out[0] = m_x[3]

    gram_far()

    @pl.when(r < peers - 1)
    def _():
        for copy in down:
            copy.wait_recv()

    curl_y = [up_out[y, pl.ds(n, n)] - below[2 * y + 1] for y in range(4)]
    curl_z = [below[2 * y] - up_out[y, pl.ds(0, n)] for y in range(4)]
    m_y = [mu_y[y] * curl_y[y] for y in range(4)]
    m_z = [mu_y[y] * curl_z[y] for y in range(4)]
    partial = partial + inner(
        jnp.concatenate(m_y + m_z, axis=1), jnp.concatenate(curl_y + curl_z, axis=1)
    )
    proj_begin(partial)
    edge_out[1] = m_z[3]

    @pl.when(c == 0)
    def _():
        edge_copy.start()

    gram_back()
    proj_near()
    gram_matrix = gram_end()
    wide_ref[...] = factor(gram_matrix)
    proj_far()

    @pl.when(c == 1)
    def _():
        edge_copy.wait_recv()

    before_x = [edge[0]] + m_x[:3]
    before_z = [edge[1]] + m_z[:3]
    for y in range(4):
        image_ref[3 * y] = (m_z[y] - before_z[y]) - backward(m_y[y]) - eps_y[y] * ex(y)

        @pl.when(r > 0)
        def _():
            up[y].wait_recv()

        lower_mu = over(up_in[y, pl.ds(2 * n, 1)])
        lower_z = lower_mu * (ey(y) - up_in[y, pl.ds(0, n)])
        lower_y = lower_mu * (up_in[y, pl.ds(n, n)] - ez(y))
        image_ref[3 * y + 1] = backward(m_x[y]) - (m_z[y] - lower_z) - eps_y[y] * ey(y)
        image_ref[3 * y + 2] = (m_y[y] - lower_y) - (m_x[y] - before_x[y]) - eps_y[y] * ez(y)

    proj_back()
    proj_ref[...] = proj_end()

    for copy in gram_used + proj_used:
        copy.wait_send()

    @pl.when(c == 1)
    def _():
        beside_copy.wait_send()

    @pl.when(c == 0)
    def _():
        edge_copy.wait_send()

    @pl.when(r > 0)
    def _():
        for copy in down:
            copy.wait_send()

    @pl.when(r < peers - 1)
    def _():
        for copy in up:
            copy.wait_send()


def last_kernel(tiles_ref, image_ref, wide_ref, proj_ref, ortho_ref, upper_ref, applied_ref, projected_ref):
    n = proj_ref.shape[0]
    wide = wide_ref[...]
    upper_ref[...] = wide[:, :n]
    inverse = wide[:, n:]
    half = times(inverse, proj_ref[...])
    projected_ref[...] = inner(half, inverse)
    for source, target in ((tiles_ref, ortho_ref), (image_ref, applied_ref)):
        for y in range(4):
            for comp in range(3):
                target[pl.ds(comp * 4 + y, n, stride=12), :] = times(inverse, source[3 * y + comp])


def local(peers, columns_of, krylov_basis, regions, mu_table, eps_table, shift_value):
    n = krylov_basis.shape[0]
    flat = krylov_basis.reshape(n * 12, 128)
    total = 3 * peers * columns_of * 4 * 128
    more = max(peers.bit_length() - 4, 0)
    copies = REDUCE + 2 * (6 + more)
    tile = (n, 128)
    vmem = pl.BlockSpec(memory_space=pltpu.VMEM)
    smem = pl.BlockSpec(memory_space=pltpu.SMEM)
    shapes = [
        jax.ShapeDtypeStruct((12,) + tile, F32),
        jax.ShapeDtypeStruct((12,) + tile, F32),
        jax.ShapeDtypeStruct((n, 2 * n), F32),
        jax.ShapeDtypeStruct((n, n), F32),
    ]
    tiles, image, wide, proj = pl.pallas_call(
        functools.partial(main_kernel, peers, total),
        out_shape=shapes,
        in_specs=[pl.BlockSpec(memory_space=pl.ANY), vmem, smem, smem, smem],
        out_specs=[vmem] * 4,
        scratch_shapes=[
            pltpu.VMEM((n * 12, 128), F32),
            pltpu.VMEM((8,) + tile, F32),
            pltpu.VMEM((3,) + tile, F32),
            pltpu.VMEM((2,) + tile, F32),
            pltpu.VMEM((2,) + tile, F32),
            pltpu.VMEM((4, 2 * n + 8, 128), F32),
            pltpu.VMEM((4, 2 * n + 8, 128), F32),
            pltpu.VMEM((2, MORE + 2 * more, n // 4, 2 * n), F32),
            pltpu.SemaphoreType.DMA,
            pltpu.SemaphoreType.DMA((copies,)),
            pltpu.SemaphoreType.DMA((copies,)),
        ],
        compiler_params=pltpu.CompilerParams(collective_id=0, has_side_effects=True, vmem_limit_bytes=32 << 20),
        name="gather_and_factor",
    )(flat, regions, mu_table, eps_table, shift_value)
    ortho, upper, applied, projected = pl.pallas_call(
        last_kernel,
        out_shape=[
            jax.ShapeDtypeStruct((n * 12, 128), F32),
            jax.ShapeDtypeStruct((n, n), F32),
            jax.ShapeDtypeStruct((n * 12, 128), F32),
            jax.ShapeDtypeStruct((n, n), F32),
        ],
        in_specs=[vmem] * 4,
        out_specs=[vmem] * 4,
        compiler_params=pltpu.CompilerParams(vmem_limit_bytes=32 << 20),
        name="multiply",
    )(tiles, image, wide, proj)
    return ortho.reshape(krylov_basis.shape), upper, applied.reshape(krylov_basis.shape), projected


def solution(mesh):
    peers = mesh.shape["row"]
    columns_of = mesh.shape["col"] * 1
    placed = (P("shift", None, "row", "col", None), P("row", "col", None), P(), P(), P("shift"))
    return jax.shard_map(
        functools.partial(local, peers, columns_of),
        mesh=mesh,
        in_specs=placed,
        out_specs=(
            P("shift", None, "row", "col", None),
            P("shift", None),
            P("shift", None, "row", "col", None),
            P("shift", None),
        ),
        check_vma=False,
    )
```

```python
import functools

import jax
import jax.numpy as jnp
from jax import lax
from jax.experimental import pallas as pl
from jax.experimental.pallas import tpu as pltpu
from jax.sharding import PartitionSpec as P

F32 = jnp.float32
BF16 = jnp.bfloat16
MESH = pl.DeviceIdType.MESH
COL, MCOPY, DOWN, UP = 0, 1, 2, 7
REDUCE = 11
GROUP = 8
PAIR_OUT, PAIR_IN, HALF, OTHER, MINE, OTHERS = 0, 1, 2, 3, 4, 5
MORE = OTHERS + GROUP - 1


def split3(x):
    high = x.astype(BF16)
    rest = x - high.astype(F32)
    mid = rest.astype(BF16)
    low = (rest - mid.astype(F32)).astype(BF16)
    return high, mid, low


def rows_dot(a, b):
    return lax.dot_general(a, b, (((1,), (1,)), ((), ())), preferred_element_type=F32)


def plain_dot(a, b):
    return lax.dot_general(a, b, (((1,), (0,)), ((), ())), preferred_element_type=F32)


def first_dot(a, b):
    return lax.dot_general(a, b, (((0,), (0,)), ((), ())), preferred_element_type=F32)


def inner(left, right=None):
    n = left.shape[0]
    a, b, c = split3(left)
    d, e, f = (a, b, c) if right is None else split3(right)
    first = rows_dot(jnp.concatenate([a, b, c], axis=0), d)
    second = rows_dot(jnp.concatenate([a, b], axis=0), e)
    third = rows_dot(a, f)
    return first[:n] + ((first[n : 2 * n] + second[:n]) + ((first[2 * n :] + third) + second[n:]))


def times(left, right):
    a, b, c = split3(left)
    d, e, f = split3(right)
    return plain_dot(
        jnp.concatenate([a, a, b, b, a, c], axis=1), jnp.concatenate([d, e, d, e, f, d], axis=0)
    )


def factor(gram):
    n = gram.shape[0]
    size = 16
    wide = 2 * n
    rows_of = lax.broadcasted_iota(jnp.int32, (n, n), 0)
    eye = (rows_of == lax.broadcasted_iota(jnp.int32, (n, n), 1)).astype(F32)
    rest = jnp.concatenate([gram, eye], axis=1)
    place = lax.broadcasted_iota(jnp.int32, (size, wide), 0)
    done, pivots = [], []
    for block in range(n // size):
        rows = rest[:size]
        begin = block * size
        cols = [
            jnp.broadcast_to(rows[:, begin + j : begin + j + 1], (size, wide)) for j in range(size)
        ]
        pivot = jnp.zeros((size, wide), F32)
        inverse = jnp.zeros((size, wide), F32)
        for k in range(size):
            head = jnp.broadcast_to(cols[k][k : k + 1], (size, wide))
            reciprocal = 1.0 / head
            pivot = jnp.where(place == k, head, pivot)
            inverse = jnp.where(place == k, reciprocal, inverse)
            if k < size - 1:
                ratio = jnp.where(place > k, cols[k] * reciprocal, 0.0)
                for j in range(k + 1, size):
                    cols[j] = cols[j] - ratio * jnp.broadcast_to(cols[j][k : k + 1], (size, wide))
                rows = rows - ratio * jnp.broadcast_to(rows[k : k + 1], (size, wide))
        done.append(rows)
        pivots.append(pivot)
        if begin + size < n:
            a, b, c = split3((rows * inverse)[:, :n])
            d, e, f = split3(rows)
            update = first_dot(
                jnp.concatenate([a, a, b, b, a, c], axis=0),
                jnp.concatenate([d, e, d, e, f, d], axis=0),
            )
            rest = rest[size:] - update[begin + size :]
    pivot = jnp.concatenate(pivots, axis=0)
    scaled = jnp.concatenate(done, axis=0) / jnp.sqrt(pivot)
    keep = lax.broadcasted_iota(jnp.int32, (n, wide), 1) >= lax.broadcasted_iota(
        jnp.int32, (n, wide), 0
    )
    return jnp.where(keep, scaled, 0.0)


def select(condition, a, b):
    return jnp.where(condition, a, b)


def main_kernel(
    peers,
    total,
    x_ref,
    regions_ref,
    mu_ref,
    eps_ref,
    shift_ref,
    tiles_ref,
    image_ref,
    wide_ref,
    proj_ref,
    landed,
    below,
    beside,
    edge,
    edge_out,
    up_out,
    up_in,
    sums,
    labels_ref,
    mu_table_ref,
    eps_table_ref,
    shift_table_ref,
    load_sem,
    send_sem,
    recv_sem,
    ready,
):
    r = lax.axis_index("row")
    c = lax.axis_index("col")
    n = landed.shape[0] // 12
    first, last = r == 0, r == peers - 1
    bits = peers.bit_length() - 1
    near = [m for m in range(1, GROUP) if m < peers]
    more = [m for m in (1 << b for b in range(bits)) if m >= GROUP]
    inside = lax.rem(r, GROUP)

    def other(mask):
        return {"row": jnp.bitwise_xor(r, mask)}

    sibling = {"col": 1 - c}
    barrier = pltpu.get_barrier_semaphore()
    pl.semaphore_signal(barrier, inc=1, device_id=sibling, device_id_type=MESH)
    for mask in more:
        pl.semaphore_signal(barrier, inc=1, device_id=other(mask), device_id_type=MESH)
    greet_lower = r > 0
    greet_upper = r < peers - 1
    size = min(GROUP, peers)
    two_lower = inside >= 2
    two_upper = inside < size - 2

    def signal_two(semaphore):
        @pl.when(two_lower)
        def _():
            pl.semaphore_signal(semaphore, inc=1, device_id={"row": r - 2}, device_id_type=MESH)

        @pl.when(two_upper)
        def _():
            pl.semaphore_signal(semaphore, inc=1, device_id={"row": r + 2}, device_id_type=MESH)

    signal_two(barrier)

    @pl.when(greet_lower)
    def _():
        pl.semaphore_signal(barrier, inc=1, device_id={"row": r - 1}, device_id_type=MESH)

    @pl.when(greet_upper)
    def _():
        pl.semaphore_signal(barrier, inc=1, device_id={"row": r + 1}, device_id_type=MESH)

    load = pltpu.make_async_copy(x_ref, landed, load_sem.at[0])
    load.start()
    small = [
        pltpu.make_async_copy(regions_ref, labels_ref, load_sem.at[1]),
        pltpu.make_async_copy(mu_ref, mu_table_ref, load_sem.at[2]),
        pltpu.make_async_copy(eps_ref, eps_table_ref, load_sem.at[3]),
        pltpu.make_async_copy(shift_ref, shift_table_ref, load_sem.at[4]),
    ]
    for copy in small:
        copy.start()

    for copy in small:
        copy.wait()
    labels = labels_ref[0]

    def entry(table, region):
        return jnp.broadcast_to(table[...][None, region : region + 1], labels.shape)

    mu = jnp.zeros(labels.shape, F32)
    eps = jnp.zeros(labels.shape, F32)
    for region in range(mu_table_ref.shape[0]):
        mu = jnp.where(labels == region, entry(mu_table_ref, region), mu)
        eps = jnp.where(labels == region, entry(eps_table_ref, region), eps)
    eps = eps * entry(shift_table_ref, 0)

    def over(row):
        return jnp.broadcast_to(row, (n, 128))

    mu_y = [over(mu[y : y + 1]) for y in range(4)]
    eps_y = [over(eps[y : y + 1]) for y in range(4)]

    load.wait()
    for y in range(4):
        for comp in range(3):
            tiles_ref[3 * y + comp] = landed[pl.ds(comp * 4 + y, n, stride=12), :]

    def remote(index, source, target, device):
        return pltpu.make_async_remote_copy(
            src_ref=source,
            dst_ref=target,
            send_sem=send_sem.at[index],
            recv_sem=recv_sem.at[index],
            device_id=device,
            device_id_type=MESH,
        )

    beside_copy = remote(COL, tiles_ref.at[pl.ds(0, 3)], beside, sibling)
    edge_copy = remote(MCOPY, edge_out, edge, sibling)
    lower = {"row": jnp.maximum(r - 1, 0)}
    upper = {"row": jnp.minimum(r + 1, peers - 1)}
    down = [
        remote(DOWN + i, tiles_ref.at[pl.ds(3 * y + 1 + k, m)], below.at[pl.ds(2 * y + k, m)], lower)
        for i, (y, k, m) in enumerate([(0, 0, 2), (1, 0, 2), (2, 0, 2), (3, 0, 1), (3, 1, 1)])
    ]
    up = []
    for y in range(4):
        part = pl.ds(0, 2 * n + 8 if y == 0 else 2 * n)
        up.append(remote(UP + y, up_out.at[y, part], up_in.at[y, part], upper))

    @pl.when(last)
    def _():
        below[...] = jnp.zeros_like(below)

    @pl.when(first)
    def _():
        up_in[...] = jnp.zeros_like(up_in)

    @pl.when(c == 1)
    def _():
        beside[...] = jnp.zeros_like(beside)

    @pl.when(c == 0)
    def _():
        edge[...] = jnp.zeros_like(edge)

    twos = jnp.where(two_lower, 1, 0) + jnp.where(two_upper, 1, 0)
    ones = jnp.where(greet_lower, 1, 0) + jnp.where(greet_upper, 1, 0)
    pl.semaphore_wait(barrier, 1 + len(more) + ones + twos)

    @pl.when(c == 1)
    def _():
        beside_copy.start()

    @pl.when(r > 0)
    def _():
        for copy in down:
            copy.start()

    def reduction(which):
        base = REDUCE + which * (GROUP + 1 + len(more))
        slot = sums.at[which]
        pair = remote(base, slot.at[PAIR_OUT], slot.at[PAIR_IN], sibling)
        back = remote(base + 1, slot.at[HALF], slot.at[OTHER], sibling)
        direct = [
            remote(base + 1 + mask, slot.at[MINE], slot.at[OTHERS + mask - 1], other(mask))
            for mask in near
        ]
        further = [
            remote(
                base + GROUP + 1 + i, slot.at[MORE + 2 * i], slot.at[MORE + 2 * i + 1], other(mask)
            )
            for i, mask in enumerate(more)
        ]

        def begin(value):
            packed = jnp.concatenate([value[: n // 2], value[n // 2 :]], axis=1)
            q = n // 4
            slot[PAIR_OUT] = jnp.where(c == 0, packed[q:], packed[:q])
            slot[MINE] = jnp.where(c == 0, packed[:q], packed[q:])
            pair.start()

        def spread():
            pair.wait_recv()
            slot[MINE] = slot[MINE] + slot[PAIR_IN]
            for copy in direct:
                copy.start()

        def collect():
            got = slot[MINE]
            for mask, copy in zip(near, direct):
                copy.wait_recv()
                got = got + slot[OTHERS + mask - 1]
            for i, copy in enumerate(further):
                slot[MORE + 2 * i] = got
                copy.start()
                copy.wait_recv()
                got = got + slot[MORE + 2 * i + 1]
            slot[HALF] = got
            back.start()

        def end():
            back.wait_recv()
            mine, theirs = slot[HALF], slot[OTHER]
            packed = jnp.concatenate(
                [jnp.where(c == 0, mine, theirs), jnp.where(c == 0, theirs, mine)], axis=0
            )
            return jnp.concatenate([packed[:, :n], packed[:, n:]], axis=0) * (1.0 / total)

        return begin, spread, collect, end, [pair, back] + direct + further

    gram_begin, gram_spread, gram_collect, gram_end, gram_used = reduction(0)
    proj_begin, proj_spread, proj_collect, proj_end, proj_used = reduction(1)

    signal_two(ready.at[0])
    every = jnp.concatenate([tiles_ref[t] for t in range(12)], axis=1)
    gram_begin(inner(every))

    lane = lax.broadcasted_iota(jnp.int32, (n, 128), 1)

    def forward(values):
        return jnp.where(lane == 127, 0.0, pltpu.roll(values, 127, 1)) - values

    def backward(values):
        return values - jnp.where(lane == 0, 0.0, pltpu.roll(values, 1, 1))

    def ex(y):
        return tiles_ref[3 * y] if y < 4 else beside[0]

    def ey(y):
        return tiles_ref[3 * y + 1]

    def ez(y):
        return tiles_ref[3 * y + 2] if y < 4 else beside[2]

    def combine(y):
        up_out[y, pl.ds(0, n)] = ey(y) + (ex(y + 1) - ex(y))
        up_out[y, pl.ds(n, n)] = ez(y) + forward(ex(y))

    up_out[0, pl.ds(2 * n, 4)] = mu
    for y in range(3):
        combine(y)

    pl.semaphore_wait(ready.at[0], twos)
    if size > 4:
        pl.semaphore_signal(ready.at[1], inc=1, device_id=other(4), device_id_type=MESH)
        pl.semaphore_wait(ready.at[1], 1)
    gram_spread()

    @pl.when(c == 0)
    def _():
        beside_copy.wait_recv()

    combine(3)

    odd = lax.rem(r, 2) == 1

    @pl.when(jnp.logical_not(odd) & (r < peers - 1))
    def _():
        for copy in up[:2]:
            copy.start()

    curl_x = [ez(y + 1) - ez(y) - forward(ey(y)) for y in range(4)]
    m_x = [mu_y[y] * curl_x[y] for y in range(4)]
    left = jnp.concatenate(
        m_x + [-eps_y[y] * tiles_ref[3 * y + comp] for y in range(4) for comp in range(3)], axis=1
    )
    right = jnp.concatenate(curl_x + [tiles_ref[t] for y in range(4) for t in range(3 * y, 3 * y + 3)], axis=1)
    partial = inner(left, right)
    edge_out[0] = m_x[3]

    curl_y, curl_z, m_y, m_z = [], [], [], []
    for y in range(4):

        @pl.when(r < peers - 1)
        def _():
            down[y].wait_recv()

        if y == 3:

            @pl.when(odd)
            def _():
                for copy in down:
                    copy.wait_send()

            @pl.when(odd & (r < peers - 1))
            def _():
                for copy in up[:2]:
                    copy.start()


            @pl.when(r < peers - 1)
            def _():
                down[4].wait_recv()

        curl_y.append(up_out[y, pl.ds(n, n)] - below[2 * y + 1])
        curl_z.append(below[2 * y] - up_out[y, pl.ds(0, n)])
        m_y.append(mu_y[y] * curl_y[y])
        m_z.append(mu_y[y] * curl_z[y])
        partial = partial + inner(
            jnp.concatenate([m_y[y], m_z[y]], axis=1), jnp.concatenate([curl_y[y], curl_z[y]], axis=1)
        )
    proj_begin(partial)
    edge_out[1] = m_z[3]

    @pl.when(c == 0)
    def _():
        edge_copy.start()

    proj_spread()

    @pl.when(r < peers - 1)
    def _():
        for copy in up[2:]:
            copy.start()

    gram_collect()
    gram_matrix = gram_end()
    wide_ref[...] = factor(gram_matrix)
    @pl.when(c == 1)
    def _():
        edge_copy.wait_recv()

    before_x = [edge[0]] + m_x[:3]
    before_z = [edge[1]] + m_z[:3]
    for y in range(4):
        if y == 3:
            proj_collect()
        image_ref[3 * y] = (m_z[y] - before_z[y]) - backward(m_y[y]) - eps_y[y] * ex(y)

        @pl.when(r > 0)
        def _():
            up[y].wait_recv()

        lower_mu = over(up_in[0, pl.ds(2 * n + y, 1)])
        lower_z = lower_mu * (ey(y) - up_in[y, pl.ds(0, n)])
        lower_y = lower_mu * (up_in[y, pl.ds(n, n)] - ez(y))
        image_ref[3 * y + 1] = backward(m_x[y]) - (m_z[y] - lower_z) - eps_y[y] * ey(y)
        image_ref[3 * y + 2] = (m_y[y] - lower_y) - (m_x[y] - before_x[y]) - eps_y[y] * ez(y)

    proj_ref[...] = proj_end()

    for copy in gram_used + proj_used:
        copy.wait_send()

    @pl.when(c == 1)
    def _():
        beside_copy.wait_send()

    @pl.when(c == 0)
    def _():
        edge_copy.wait_send()

    @pl.when((r > 0) & jnp.logical_not(odd))
    def _():
        for copy in down:
            copy.wait_send()

    @pl.when(r < peers - 1)
    def _():
        for copy in up:
            copy.wait_send()


def last_kernel(tiles_ref, image_ref, wide_ref, proj_ref, ortho_ref, upper_ref, applied_ref, projected_ref):
    n = proj_ref.shape[0]
    wide = wide_ref[...]
    upper_ref[...] = wide[:, :n]
    inverse = wide[:, n:]
    half = times(inverse, proj_ref[...])
    projected_ref[...] = inner(half, inverse)
    for source, target in ((tiles_ref, ortho_ref), (image_ref, applied_ref)):
        for y in range(4):
            for comp in range(3):
                target[pl.ds(comp * 4 + y, n, stride=12), :] = times(inverse, source[3 * y + comp])


def local(peers, columns_of, krylov_basis, regions, mu_table, eps_table, shift_value):
    n = krylov_basis.shape[0]
    flat = krylov_basis.reshape(n * 12, 128)
    total = 3 * peers * columns_of * 4 * 128
    more = max(peers.bit_length() - 4, 0)
    copies = REDUCE + 2 * (GROUP + 1 + more)
    tile = (n, 128)
    vmem = pl.BlockSpec(memory_space=pltpu.VMEM)
    shapes = [
        jax.ShapeDtypeStruct((12,) + tile, F32),
        jax.ShapeDtypeStruct((12,) + tile, F32),
        jax.ShapeDtypeStruct((n, 2 * n), F32),
        jax.ShapeDtypeStruct((n, n), F32),
    ]
    tiles, image, wide, proj = pl.pallas_call(
        functools.partial(main_kernel, peers, total),
        out_shape=shapes,
        in_specs=[pl.BlockSpec(memory_space=pltpu.HBM)] * 5,
        out_specs=[vmem] * 4,
        scratch_shapes=[
            pltpu.VMEM((n * 12, 128), F32),
            pltpu.VMEM((8,) + tile, F32),
            pltpu.VMEM((3,) + tile, F32),
            pltpu.VMEM((2,) + tile, F32),
            pltpu.VMEM((2,) + tile, F32),
            pltpu.VMEM((4, 2 * n + 8, 128), F32),
            pltpu.VMEM((4, 2 * n + 8, 128), F32),
            pltpu.VMEM((2, MORE + 2 * more, n // 4, 2 * n), F32),
            pltpu.VMEM(regions.shape, regions.dtype),
            pltpu.VMEM(mu_table.shape, F32),
            pltpu.VMEM(eps_table.shape, F32),
            pltpu.VMEM(shift_value.shape, F32),
            pltpu.SemaphoreType.DMA((5,)),
            pltpu.SemaphoreType.DMA((copies,)),
            pltpu.SemaphoreType.DMA((copies,)),
            pltpu.SemaphoreType.REGULAR((2,)),
        ],
        compiler_params=pltpu.CompilerParams(collective_id=0, has_side_effects=True, vmem_limit_bytes=32 << 20),
        name="gather_and_factor",
    )(
        *(pltpu.with_memory_space_constraint(array, pltpu.HBM) for array in (flat, regions, mu_table, eps_table)),
        shift_value,
    )
    ortho, upper, applied, projected = pl.pallas_call(
        last_kernel,
        out_shape=[
            jax.ShapeDtypeStruct((n * 12, 128), F32),
            jax.ShapeDtypeStruct((n, n), F32),
            jax.ShapeDtypeStruct((n * 12, 128), F32),
            jax.ShapeDtypeStruct((n, n), F32),
        ],
        in_specs=[vmem] * 4,
        out_specs=[vmem] * 4,
        compiler_params=pltpu.CompilerParams(vmem_limit_bytes=32 << 20),
        name="multiply",
    )(tiles, image, wide, proj)
    return ortho.reshape(krylov_basis.shape), upper, applied.reshape(krylov_basis.shape), projected


def solution(mesh):
    peers = mesh.shape["row"]
    columns_of = mesh.shape["col"] * 1
    placed = (P("shift", None, "row", "col", None), P("row", "col", None), P(), P(), P("shift"))
    return jax.shard_map(
        functools.partial(local, peers, columns_of),
        mesh=mesh,
        in_specs=placed,
        out_specs=(
            P("shift", None, "row", "col", None),
            P("shift", None),
            P("shift", None, "row", "col", None),
            P("shift", None),
        ),
        check_vma=False,
    )
```

```python
import functools

import jax
import jax.numpy as jnp
from jax import lax
from jax.experimental import pallas as pl
from jax.experimental.pallas import tpu as pltpu
from jax.sharding import PartitionSpec as P

F32 = jnp.float32
BF16 = jnp.bfloat16
MESH = pl.DeviceIdType.MESH
SIDE, DOWN, UP = 0, 1, 6
REDUCE = 10
BELOW, ABOVE, SUMS, FURTHER = 1, 2, 3, 4
GROUP = 8
PAIR_OUT, PAIR_IN, HALF, OTHER, MINE, OTHERS = 0, 1, 2, 3, 4, 5
MORE = OTHERS + GROUP - 1


def split3(x):
    high = x.astype(BF16)
    rest = x - high.astype(F32)
    mid = rest.astype(BF16)
    low = (rest - mid.astype(F32)).astype(BF16)
    return high, mid, low


def rows_dot(a, b):
    return lax.dot_general(a, b, (((1,), (1,)), ((), ())), preferred_element_type=F32)


def plain_dot(a, b):
    return lax.dot_general(a, b, (((1,), (0,)), ((), ())), preferred_element_type=F32)


def first_dot(a, b):
    return lax.dot_general(a, b, (((0,), (0,)), ((), ())), preferred_element_type=F32)


def inner(left, right=None):
    n = left.shape[0]
    a, b, c = split3(left)
    d, e, f = (a, b, c) if right is None else split3(right)
    first = rows_dot(jnp.concatenate([a, b, c], axis=0), d)
    second = rows_dot(jnp.concatenate([a, b], axis=0), e)
    third = rows_dot(a, f)
    return first[:n] + ((first[n : 2 * n] + second[:n]) + ((first[2 * n :] + third) + second[n:]))


def left_terms(left):
    a, b, c = split3(left)
    return jnp.concatenate([a, a, b, b, a, c], axis=1)


def times(left, right):
    d, e, f = split3(right)
    return plain_dot(left, jnp.concatenate([d, e, d, e, f, d], axis=0))


def factor(gram):
    n = gram.shape[0]
    size = 16
    wide = 2 * n
    rows_of = lax.broadcasted_iota(jnp.int32, (n, n), 0)
    eye = (rows_of == lax.broadcasted_iota(jnp.int32, (n, n), 1)).astype(F32)
    rest = jnp.concatenate([gram, eye], axis=1)
    place = lax.broadcasted_iota(jnp.int32, (size, wide), 0)
    done, pivots = [], []
    for block in range(n // size):
        rows = rest[:size]
        begin = block * size
        cols = [
            jnp.broadcast_to(rows[:, begin + j : begin + j + 1], (size, wide)) for j in range(size)
        ]
        pivot = jnp.zeros((size, wide), F32)
        inverse = jnp.zeros((size, wide), F32)
        for k in range(size):
            head = jnp.broadcast_to(cols[k][k : k + 1], (size, wide))
            reciprocal = 1.0 / head
            pivot = jnp.where(place == k, head, pivot)
            inverse = jnp.where(place == k, reciprocal, inverse)
            if k < size - 1:
                ratio = jnp.where(place > k, cols[k] * reciprocal, 0.0)
                for j in range(k + 1, size):
                    cols[j] = cols[j] - ratio * jnp.broadcast_to(cols[j][k : k + 1], (size, wide))
                rows = rows - ratio * jnp.broadcast_to(rows[k : k + 1], (size, wide))
        done.append(rows)
        pivots.append(pivot)
        if begin + size < n:
            a, b, c = split3((rows * inverse)[:, :n])
            d, e, f = split3(rows)
            update = first_dot(
                jnp.concatenate([a, a, b, b, a, c], axis=0),
                jnp.concatenate([d, e, d, e, f, d], axis=0),
            )
            rest = rest[size:] - update[begin + size :]
    pivot = jnp.concatenate(pivots, axis=0)
    scaled = jnp.concatenate(done, axis=0) / jnp.sqrt(pivot)
    keep = lax.broadcasted_iota(jnp.int32, (n, wide), 1) >= lax.broadcasted_iota(
        jnp.int32, (n, wide), 0
    )
    return jnp.where(keep, scaled, 0.0)


def select(condition, a, b):
    return jnp.where(condition, a, b)


def main_kernel(
    peers,
    total,
    x_ref,
    regions_ref,
    mu_ref,
    eps_ref,
    shift_ref,
    ortho_ref,
    upper_ref,
    applied_ref,
    projected_ref,
    tiles_ref,
    landed,
    below,
    beside,
    edge,
    edge_out,
    up_out,
    up_in,
    sums,
    labels_ref,
    mu_table_ref,
    eps_table_ref,
    shift_table_ref,
    load_sem,
    send_sem,
    recv_sem,
    ready,
):
    r = lax.axis_index("row")
    c = lax.axis_index("col")
    n = landed.shape[0] // 12
    first, last = r == 0, r == peers - 1
    bits = peers.bit_length() - 1
    near = [m for m in range(1, GROUP) if m < peers]
    more = [m for m in (1 << b for b in range(bits)) if m >= GROUP]
    inside = lax.rem(r, GROUP)

    def other(mask):
        return {"row": jnp.bitwise_xor(r, mask)}

    sibling = {"col": 1 - c}
    load = pltpu.make_async_copy(x_ref, landed, load_sem.at[0])
    load.start()

    size = min(GROUP, peers)
    lower_two, upper_two = inside >= 2, inside < size - 2
    barrier = pltpu.get_barrier_semaphore()

    def greet(semaphore, condition, step):
        @pl.when(condition)
        def _():
            pl.semaphore_signal(semaphore, inc=1, device_id={"row": r + step}, device_id_type=MESH)

    def count(*conditions):
        return sum(jnp.where(condition, 1, 0) for condition in conditions)

    pl.semaphore_signal(barrier, inc=1, device_id=sibling, device_id_type=MESH)
    for mask in more:
        pl.semaphore_signal(barrier, inc=1, device_id=other(mask), device_id_type=MESH)
    greet(barrier, r < peers - 1, 1)
    greet(barrier, upper_two, 2)

    small = [
        pltpu.make_async_copy(regions_ref, labels_ref, load_sem.at[1]),
        pltpu.make_async_copy(mu_ref, mu_table_ref, load_sem.at[2]),
        pltpu.make_async_copy(eps_ref, eps_table_ref, load_sem.at[3]),
        pltpu.make_async_copy(shift_ref, shift_table_ref, load_sem.at[4]),
    ]
    for copy in small:
        copy.start()

    for copy in small:
        copy.wait()
    labels = labels_ref[0]

    def entry(table, region):
        return jnp.broadcast_to(table[...][None, region : region + 1], labels.shape)

    mu = jnp.zeros(labels.shape, F32)
    eps = jnp.zeros(labels.shape, F32)
    for region in range(mu_table_ref.shape[0]):
        mu = jnp.where(labels == region, entry(mu_table_ref, region), mu)
        eps = jnp.where(labels == region, entry(eps_table_ref, region), eps)
    eps = eps * entry(shift_table_ref, 0)

    def over(row):
        return jnp.broadcast_to(row, (n, 128))

    mu_y = [over(mu[y : y + 1]) for y in range(4)]
    eps_y = [over(eps[y : y + 1]) for y in range(4)]

    load.wait()
    for y in range(4):
        for comp in range(3):
            tiles_ref[3 * y + comp] = landed[pl.ds(comp * 4 + y, n, stride=12), :]

    def remote(sent, index, source, target, device):
        return pltpu.make_async_remote_copy(
            src_ref=source,
            dst_ref=target,
            send_sem=send_sem.at[sent],
            recv_sem=recv_sem.at[index],
            device_id=device,
            device_id_type=MESH,
        )

    def sent_all(sent, like):
        remote(sent, 0, like, like, sibling).wait_send()

    beside_copy = remote(SIDE, SIDE, tiles_ref.at[pl.ds(0, 3)], beside, sibling)
    edge_copy = remote(SIDE, SIDE, edge_out, edge, sibling)
    lower = {"row": jnp.maximum(r - 1, 0)}
    upper = {"row": jnp.minimum(r + 1, peers - 1)}
    down = [
        remote(BELOW, DOWN + i, tiles_ref.at[pl.ds(3 * y + 1 + k, m)], below.at[pl.ds(2 * y + k, m)], lower)
        for i, (y, k, m) in enumerate([(0, 0, 2), (1, 0, 2), (2, 0, 2), (3, 0, 1), (3, 1, 1)])
    ]
    up = []
    for y in range(4):
        part = pl.ds(0, 2 * n + 8 if y == 0 else 2 * n)
        up.append(remote(ABOVE, UP + y, up_out.at[y, part], up_in.at[y, part], upper))

    @pl.when(last)
    def _():
        below[...] = jnp.zeros_like(below)

    @pl.when(first)
    def _():
        up_in[...] = jnp.zeros_like(up_in)

    @pl.when(c == 1)
    def _():
        beside[...] = jnp.zeros_like(beside)

    @pl.when(c == 0)
    def _():
        edge[...] = jnp.zeros_like(edge)

    pl.semaphore_wait(barrier, 1 + len(more) + count(r > 0, lower_two))
    @pl.when(c == 1)
    def _():
        beside_copy.start()

    @pl.when(r > 0)
    def _():
        for copy in down:
            copy.start()

    def reduction(which):
        base = REDUCE + which * (3 + len(more))
        slot = sums.at[which]
        pair = remote(SUMS, base, slot.at[PAIR_OUT], slot.at[PAIR_IN], sibling)
        back = remote(SUMS, base + 1, slot.at[HALF], slot.at[OTHER], sibling)
        direct = [
            remote(SUMS, base + 2, slot.at[MINE], slot.at[OTHERS + mask - 1], other(mask))
            for mask in near
        ]
        everyone = slot.at[pl.ds(OTHERS, len(near))]
        arrived = remote(SUMS, base + 2, everyone, everyone, sibling)
        further = [
            remote(
                FURTHER + which * len(more) + i,
                base + 3 + i,
                slot.at[MORE + 2 * i],
                slot.at[MORE + 2 * i + 1],
                other(mask),
            )
            for i, mask in enumerate(more)
        ]

        def begin(value):
            packed = jnp.concatenate([value[: n // 2], value[n // 2 :]], axis=1)
            q = n // 4
            slot[PAIR_OUT] = jnp.where(c == 0, packed[q:], packed[:q])
            slot[MINE] = jnp.where(c == 0, packed[:q], packed[q:])
            pair.start()

        def spread():
            pair.wait_recv()
            slot[MINE] = slot[MINE] + slot[PAIR_IN]
            for copy in direct:
                copy.start()

        def collect():
            got = slot[MINE]
            arrived.wait_recv()
            for mask in near:
                got = got + slot[OTHERS + mask - 1]
            for i, copy in enumerate(further):
                slot[MORE + 2 * i] = got
                copy.start()
                copy.wait_recv()
                got = got + slot[MORE + 2 * i + 1]
            slot[HALF] = got
            back.start()

        def end():
            back.wait_recv()
            mine, theirs = slot[HALF], slot[OTHER]
            packed = jnp.concatenate(
                [jnp.where(c == 0, mine, theirs), jnp.where(c == 0, theirs, mine)], axis=0
            )
            return jnp.concatenate([packed[:, :n], packed[:, n:]], axis=0) * (1.0 / total)

        return begin, spread, collect, end, further

    gram_begin, gram_spread, gram_collect, gram_end, gram_used = reduction(0)
    proj_begin, proj_spread, proj_collect, proj_end, proj_used = reduction(1)

    greet(ready.at[0], r > 0, -1)
    greet(ready.at[0], lower_two, -2)
    every = jnp.concatenate([tiles_ref[t] for t in range(12)], axis=1)
    gram_begin(inner(every))

    lane = lax.broadcasted_iota(jnp.int32, (n, 128), 1)

    def forward(values):
        return jnp.where(lane == 127, 0.0, pltpu.roll(values, 127, 1)) - values

    def backward(values):
        return values - jnp.where(lane == 0, 0.0, pltpu.roll(values, 1, 1))

    def ex(y):
        return tiles_ref[3 * y] if y < 4 else beside[0]

    def ey(y):
        return tiles_ref[3 * y + 1]

    def ez(y):
        return tiles_ref[3 * y + 2] if y < 4 else beside[2]

    def combine(y):
        up_out[y, pl.ds(0, n)] = ey(y) + (ex(y + 1) - ex(y))
        up_out[y, pl.ds(n, n)] = ez(y) + forward(ex(y))

    up_out[0, pl.ds(2 * n, 4)] = mu
    for y in range(3):
        combine(y)

    @pl.when(r < peers - 1)
    def _():
        pl.semaphore_wait(ready.at[0], count(r < peers - 1, upper_two))

    greet(ready.at[1], lower_two, -2)
    greet(ready.at[1], upper_two, 2)

    @pl.when(lower_two | upper_two)
    def _():
        pl.semaphore_wait(ready.at[1], count(lower_two, upper_two))

    if size > 4:
        pl.semaphore_signal(ready.at[2], inc=1, device_id=other(4), device_id_type=MESH)
        pl.semaphore_wait(ready.at[2], 1)
    gram_spread()

    @pl.when(c == 0)
    def _():
        beside_copy.wait_recv()

    combine(3)

    odd = lax.rem(r, 2) == 1

    @pl.when(jnp.logical_not(odd) & (r < peers - 1))
    def _():
        for copy in up[:2]:
            copy.start()

    curl_x = [ez(y + 1) - ez(y) - forward(ey(y)) for y in range(4)]
    m_x = [mu_y[y] * curl_x[y] for y in range(4)]
    left = jnp.concatenate(
        m_x + [-eps_y[y] * tiles_ref[3 * y + comp] for y in range(4) for comp in range(3)], axis=1
    )
    right = jnp.concatenate(curl_x + [tiles_ref[t] for y in range(4) for t in range(3 * y, 3 * y + 3)], axis=1)
    partial = inner(left, right)
    edge_out[0] = m_x[3]

    curl_y, curl_z, m_y, m_z = [], [], [], []
    for y in range(4):

        @pl.when(r < peers - 1)
        def _():
            down[y].wait_recv()

        if y == 3:

            @pl.when(odd)
            def _():
                sent_all(BELOW, below)

            @pl.when(odd & (r < peers - 1))
            def _():
                for copy in up[:2]:
                    copy.start()


            @pl.when(r < peers - 1)
            def _():
                down[4].wait_recv()

        curl_y.append(up_out[y, pl.ds(n, n)] - below[2 * y + 1])
        curl_z.append(below[2 * y] - up_out[y, pl.ds(0, n)])
        m_y.append(mu_y[y] * curl_y[y])
        m_z.append(mu_y[y] * curl_z[y])
        partial = partial + inner(
            jnp.concatenate([m_y[y], m_z[y]], axis=1), jnp.concatenate([curl_y[y], curl_z[y]], axis=1)
        )
    proj_begin(partial)
    edge_out[1] = m_z[3]

    @pl.when(c == 0)
    def _():
        edge_copy.start()

    proj_spread()

    @pl.when(r < peers - 1)
    def _():
        for copy in up[2:]:
            copy.start()

    gram_collect()
    gram_matrix = gram_end()
    wide = factor(gram_matrix)
    upper_ref[...] = wide[:, :n]
    inverse = wide[:, n:]
    left = left_terms(inverse)

    def put(target, y, comp, value):
        target[pl.ds(comp * 4 + y, n, stride=12), :] = times(left, value)

    for place in range(12):
        put(ortho_ref, place // 3, place % 3, tiles_ref[place])

    proj_collect()

    @pl.when(c == 1)
    def _():
        edge_copy.wait_recv()


    @pl.when(r > 0)
    def _():
        for copy in up[:3]:
            copy.wait_recv()

    before_x = [edge[0]] + m_x[:3]
    before_z = [edge[1]] + m_z[:3]

    def finish(y):
        lower_mu = over(up_in[0, pl.ds(2 * n + y, 1)])
        lower_z = lower_mu * (ey(y) - up_in[y, pl.ds(0, n)])
        lower_y = lower_mu * (up_in[y, pl.ds(n, n)] - ez(y))
        image_y = backward(m_x[y]) - (m_z[y] - lower_z) - eps_y[y] * ey(y)
        image_z = (m_y[y] - lower_y) - (m_x[y] - before_x[y]) - eps_y[y] * ez(y)
        put(applied_ref, y, 1, image_y)
        put(applied_ref, y, 2, image_z)

    for y in range(4):
        image_x = (m_z[y] - before_z[y]) - backward(m_y[y]) - eps_y[y] * ex(y)
        put(applied_ref, y, 0, image_x)
    for y in range(3):
        finish(y)

    @pl.when(first)
    def _():
        finish(3)

    half = times(left, proj_end())
    projected_ref[...] = inner(half, inverse)

    @pl.when(r > 0)
    def _():
        up[3].wait_recv()
        finish(3)

    for copy in gram_used + proj_used:
        copy.wait_send()
    sent_all(SUMS, sums.at[:, pl.ds(0, len(near) + 2)])

    @pl.when(c == 1)
    def _():
        beside_copy.wait_send()

    @pl.when(c == 0)
    def _():
        edge_copy.wait_send()

    @pl.when((r > 0) & jnp.logical_not(odd))
    def _():
        sent_all(BELOW, below)

    @pl.when(r < peers - 1)
    def _():
        sent_all(ABOVE, landed.at[pl.ds(0, 8 * n + 8)])


def last_kernel(*refs):
    sources, targets, semaphores = refs[:4], refs[4:8], refs[8]
    copies = [
        pltpu.make_async_copy(source, target, semaphores.at[i])
        for i, (source, target) in enumerate(zip(sources, targets))
    ]
    for copy in copies:
        copy.start()
    for copy in copies:
        copy.wait()


def local(peers, columns_of, krylov_basis, regions, mu_table, eps_table, shift_value):
    n = krylov_basis.shape[0]
    flat = krylov_basis.reshape(n * 12, 128)
    total = 3 * peers * columns_of * 4 * 128
    more = max(peers.bit_length() - 4, 0)
    received = REDUCE + 2 * (3 + more)
    sent = FURTHER + 2 * more
    tile = (n, 128)
    vmem = pl.BlockSpec(memory_space=pltpu.VMEM)
    shapes = [
        jax.ShapeDtypeStruct((n * 12, 128), F32),
        jax.ShapeDtypeStruct((n, n), F32),
        jax.ShapeDtypeStruct((n * 12, 128), F32),
        jax.ShapeDtypeStruct((n, n), F32),
    ]
    results = pl.pallas_call(
        functools.partial(main_kernel, peers, total),
        out_shape=shapes,
        in_specs=[pl.BlockSpec(memory_space=pltpu.HBM)] * 5,
        out_specs=[vmem] * 4,
        scratch_shapes=[
            pltpu.VMEM((12,) + tile, F32),
            pltpu.VMEM((n * 12, 128), F32),
            pltpu.VMEM((8,) + tile, F32),
            pltpu.VMEM((3,) + tile, F32),
            pltpu.VMEM((2,) + tile, F32),
            pltpu.VMEM((2,) + tile, F32),
            pltpu.VMEM((4, 2 * n + 8, 128), F32),
            pltpu.VMEM((4, 2 * n + 8, 128), F32),
            pltpu.VMEM((2, MORE + 2 * more, n // 4, 2 * n), F32),
            pltpu.VMEM(regions.shape, regions.dtype),
            pltpu.VMEM(mu_table.shape, F32),
            pltpu.VMEM(eps_table.shape, F32),
            pltpu.VMEM(shift_value.shape, F32),
            pltpu.SemaphoreType.DMA((5,)),
            pltpu.SemaphoreType.DMA((sent,)),
            pltpu.SemaphoreType.DMA((received,)),
            pltpu.SemaphoreType.REGULAR((3,)),
        ],
        compiler_params=pltpu.CompilerParams(collective_id=0, has_side_effects=True, vmem_limit_bytes=32 << 20),
        name="gather_and_factor",
    )(
        *(pltpu.with_memory_space_constraint(array, pltpu.HBM) for array in (flat, regions, mu_table, eps_table)),
        shift_value,
    )
    ortho, upper, applied, projected = pl.pallas_call(
        last_kernel,
        out_shape=shapes,
        in_specs=[vmem] * 4,
        out_specs=[pl.BlockSpec(memory_space=pl.ANY)] * 4,
        scratch_shapes=[pltpu.SemaphoreType.DMA((4,))],
        compiler_params=pltpu.CompilerParams(vmem_limit_bytes=16 << 20),
        name="hand_over",
    )(*results)
    return ortho.reshape(krylov_basis.shape), upper, applied.reshape(krylov_basis.shape), projected


def solution(mesh):
    peers = mesh.shape["row"]
    columns_of = mesh.shape["col"] * 1
    placed = (P("shift", None, "row", "col", None), P("row", "col", None), P(), P(), P("shift"))
    return jax.shard_map(
        functools.partial(local, peers, columns_of),
        mesh=mesh,
        in_specs=placed,
        out_specs=(
            P("shift", None, "row", "col", None),
            P("shift", None),
            P("shift", None, "row", "col", None),
            P("shift", None),
        ),
        check_vma=False,
    )
```

```python
import functools

import jax
import jax.numpy as jnp
from jax import lax
from jax.experimental import pallas as pl
from jax.experimental.pallas import tpu as pltpu
from jax.sharding import PartitionSpec as P

F32 = jnp.float32
BF16 = jnp.bfloat16
MESH = pl.DeviceIdType.MESH
SIDE, DOWN, UP = 0, 1, 6
REDUCE = 10
BELOW, ABOVE, SUMS, FURTHER = 1, 2, 3, 4
GROUP = 8
PAIR_OUT, PAIR_IN, HALF, OTHER, MINE, OTHERS = 0, 1, 2, 3, 4, 5
ACROSS = OTHERS + GROUP - 1
MORE = ACROSS + GROUP


def split3(x):
    high = x.astype(BF16)
    rest = x - high.astype(F32)
    mid = rest.astype(BF16)
    low = (rest - mid.astype(F32)).astype(BF16)
    return high, mid, low


def rows_dot(a, b):
    return lax.dot_general(a, b, (((1,), (1,)), ((), ())), preferred_element_type=F32)


def plain_dot(a, b):
    return lax.dot_general(a, b, (((1,), (0,)), ((), ())), preferred_element_type=F32)


def first_dot(a, b):
    return lax.dot_general(a, b, (((0,), (0,)), ((), ())), preferred_element_type=F32)


def inner(left, right=None):
    n = left.shape[0]
    a, b, c = split3(left)
    d, e, f = (a, b, c) if right is None else split3(right)
    first = rows_dot(jnp.concatenate([a, b, c], axis=0), d)
    second = rows_dot(jnp.concatenate([a, b], axis=0), e)
    third = rows_dot(a, f)
    return first[:n] + ((first[n : 2 * n] + second[:n]) + ((first[2 * n :] + third) + second[n:]))


def left_terms(left):
    a, b, c = split3(left)
    return jnp.concatenate([a, a, b, b, a, c], axis=1)


def times(left, right):
    d, e, f = split3(right)
    return plain_dot(left, jnp.concatenate([d, e, d, e, f, d], axis=0))


def factor(gram):
    n = gram.shape[0]
    size = 16
    wide = 2 * n
    rows_of = lax.broadcasted_iota(jnp.int32, (n, n), 0)
    eye = (rows_of == lax.broadcasted_iota(jnp.int32, (n, n), 1)).astype(F32)
    rest = jnp.concatenate([gram, eye], axis=1)
    place = lax.broadcasted_iota(jnp.int32, (size, wide), 0)
    done, pivots = [], []
    for block in range(n // size):
        rows = rest[:size]
        begin = block * size
        cols = [
            jnp.broadcast_to(rows[:, begin + j : begin + j + 1], (size, wide)) for j in range(size)
        ]
        pivot = jnp.zeros((size, wide), F32)
        inverse = jnp.zeros((size, wide), F32)
        for k in range(size):
            head = jnp.broadcast_to(cols[k][k : k + 1], (size, wide))
            reciprocal = 1.0 / head
            pivot = jnp.where(place == k, head, pivot)
            inverse = jnp.where(place == k, reciprocal, inverse)
            if k < size - 1:
                ratio = jnp.where(place > k, cols[k] * reciprocal, 0.0)
                for j in range(k + 1, size):
                    cols[j] = cols[j] - ratio * jnp.broadcast_to(cols[j][k : k + 1], (size, wide))
                rows = rows - ratio * jnp.broadcast_to(rows[k : k + 1], (size, wide))
        done.append(rows)
        pivots.append(pivot)
        if begin + size < n:
            a, b, c = split3((rows * inverse)[:, :n])
            d, e, f = split3(rows)
            update = first_dot(
                jnp.concatenate([a, a, b, b, a, c], axis=0),
                jnp.concatenate([d, e, d, e, f, d], axis=0),
            )
            rest = rest[size:] - update[begin + size :]
    pivot = jnp.concatenate(pivots, axis=0)
    scaled = jnp.concatenate(done, axis=0) / jnp.sqrt(pivot)
    keep = lax.broadcasted_iota(jnp.int32, (n, wide), 1) >= lax.broadcasted_iota(
        jnp.int32, (n, wide), 0
    )
    return jnp.where(keep, scaled, 0.0)


def main_kernel(
    peers,
    total,
    x_ref,
    regions_ref,
    mu_ref,
    eps_ref,
    shift_ref,
    ortho_ref,
    upper_ref,
    applied_ref,
    projected_ref,
    tiles_ref,
    landed,
    below,
    beside,
    edge,
    edge_out,
    up_out,
    up_in,
    sums,
    labels_ref,
    mu_table_ref,
    eps_table_ref,
    shift_table_ref,
    load_sem,
    send_sem,
    recv_sem,
    ready,
):
    r = lax.axis_index("row")
    c = lax.axis_index("col")
    n = landed.shape[0] // 12
    first, last = r == 0, r == peers - 1
    bits = peers.bit_length() - 1
    near = [m for m in range(1, GROUP) if m < peers]
    more = [m for m in (1 << b for b in range(bits)) if m >= GROUP]
    inside = lax.rem(r, GROUP)
    single = peers == GROUP
    exchange = jnp.logical_not(first) if single else r >= 0

    def other(mask):
        return {"row": jnp.bitwise_xor(r, mask)}

    sibling = {"col": 1 - c}
    load = pltpu.make_async_copy(x_ref, landed, load_sem.at[0])
    load.start()

    size = min(GROUP, peers)
    lower_two, upper_two = inside >= 2, inside < size - 2
    barrier = pltpu.get_barrier_semaphore()

    def greet(semaphore, condition, step):
        @pl.when(condition)
        def _():
            pl.semaphore_signal(semaphore, inc=1, device_id={"row": r + step}, device_id_type=MESH)

    def count(*conditions):
        return sum(jnp.where(condition, 1, 0) for condition in conditions)

    pl.semaphore_signal(barrier, inc=1, device_id=sibling, device_id_type=MESH)
    for mask in more:
        pl.semaphore_signal(barrier, inc=1, device_id=other(mask), device_id_type=MESH)
    greet(barrier, r < peers - 1, 1)
    greet(barrier, upper_two, 2)

    small = [
        pltpu.make_async_copy(regions_ref, labels_ref, load_sem.at[1]),
        pltpu.make_async_copy(mu_ref, mu_table_ref, load_sem.at[2]),
        pltpu.make_async_copy(eps_ref, eps_table_ref, load_sem.at[3]),
        pltpu.make_async_copy(shift_ref, shift_table_ref, load_sem.at[4]),
    ]
    for copy in small:
        copy.start()

    load.wait()
    for y in range(4):
        for comp in range(3):
            tiles_ref[3 * y + comp] = landed[pl.ds(comp * 4 + y, n, stride=12), :]

    def remote(sent, index, source, target, device):
        return pltpu.make_async_remote_copy(
            src_ref=source,
            dst_ref=target,
            send_sem=send_sem.at[sent],
            recv_sem=recv_sem.at[index],
            device_id=device,
            device_id_type=MESH,
        )

    def sent_all(sent, like):
        remote(sent, 0, like, like, sibling).wait_send()

    beside_copy = remote(SIDE, SIDE, tiles_ref.at[pl.ds(0, 3)], beside, sibling)
    edge_copy = remote(SIDE, SIDE, edge_out, edge, sibling)
    lower = {"row": jnp.maximum(r - 1, 0)}
    upper = {"row": jnp.minimum(r + 1, peers - 1)}
    down = [
        remote(BELOW, DOWN + i, tiles_ref.at[pl.ds(3 * y + 1 + k, m)], below.at[pl.ds(2 * y + k, m)], lower)
        for i, (y, k, m) in enumerate([(0, 0, 2), (1, 0, 2), (2, 0, 2), (3, 0, 1), (3, 1, 1)])
    ]
    up = []
    for y in range(4):
        part = pl.ds(0, 2 * n + 8 if y == 0 else 2 * n)
        up.append(remote(ABOVE, UP + y, up_out.at[y, part], up_in.at[y, part], upper))

    @pl.when(last)
    def _():
        below[...] = jnp.zeros_like(below)

    @pl.when(first)
    def _():
        up_in[...] = jnp.zeros_like(up_in)

    @pl.when(c == 1)
    def _():
        beside[...] = jnp.zeros_like(beside)

    @pl.when(c == 0)
    def _():
        edge[...] = jnp.zeros_like(edge)

    pl.semaphore_wait(barrier, 1 + len(more) + count(r > 0, lower_two))
    @pl.when(c == 1)
    def _():
        beside_copy.start()

    @pl.when(r > 0)
    def _():
        for copy in down:
            copy.start()

    for copy in small:
        copy.wait()
    labels = labels_ref[0]

    def entry(table, region):
        return jnp.broadcast_to(table[...][None, region : region + 1], labels.shape)

    mu = jnp.zeros(labels.shape, F32)
    eps = jnp.zeros(labels.shape, F32)
    for region in range(mu_table_ref.shape[0]):
        mu = jnp.where(labels == region, entry(mu_table_ref, region), mu)
        eps = jnp.where(labels == region, entry(eps_table_ref, region), eps)
    eps = eps * entry(shift_table_ref, 0)

    def over(row):
        return jnp.broadcast_to(row, (n, 128))

    mu_y = [over(mu[y : y + 1]) for y in range(4)]
    eps_y = [over(eps[y : y + 1]) for y in range(4)]

    def reduction(which):
        base = REDUCE + which * (4 + len(more))
        slot = sums.at[which]
        both = single and which == 1
        swap = exchange if both else r >= 0
        pair = remote(SUMS, base, slot.at[PAIR_OUT], slot.at[PAIR_IN], sibling)
        back = remote(SUMS, base + 1, slot.at[HALF], slot.at[OTHER], sibling)
        direct = [
            remote(SUMS, base + 2, slot.at[MINE], slot.at[OTHERS + mask - 1], other(mask))
            for mask in near
        ]
        everyone = slot.at[pl.ds(OTHERS, len(near))]
        arrived = remote(SUMS, base + 2, everyone, everyone, sibling)
        further = [
            remote(
                FURTHER + which * len(more) + i,
                base + 4 + i,
                slot.at[MORE + 2 * i],
                slot.at[MORE + 2 * i + 1],
                other(mask),
            )
            for i, mask in enumerate(more)
        ]

        across = both and remote(
            SUMS,
            base + 3,
            slot.at[MINE],
            slot.at[ACROSS + lax.rem(r + GROUP - 1, GROUP)],
            {"row": 0, "col": 1 - c},
        )
        everything = slot.at[pl.ds(ACROSS, GROUP)]
        gathered = both and remote(SUMS, base + 3, everything, everything, sibling)

        def begin(value):
            packed = jnp.concatenate([value[: n // 2], value[n // 2 :]], axis=1)
            q = n // 4
            slot[PAIR_OUT] = jnp.where(c == 0, packed[q:], packed[:q])
            slot[MINE] = jnp.where(c == 0, packed[:q], packed[q:])
            pair.start()

        def spread():
            pair.wait_recv()
            slot[MINE] = slot[MINE] + slot[PAIR_IN]
            for copy in direct:
                copy.start()
            if both:
                across.start()

        def collect():
            got = slot[MINE]
            arrived.wait_recv()
            for mask in near:
                got = got + slot[OTHERS + mask - 1]
            for i, copy in enumerate(further):
                slot[MORE + 2 * i] = got
                copy.start()
                copy.wait_recv()
                got = got + slot[MORE + 2 * i + 1]
            slot[HALF] = got

            @pl.when(swap)
            def _():
                back.start()

        def end():
            @pl.when(swap)
            def _():
                back.wait_recv()

            if both:

                @pl.when(first)
                def _():
                    gathered.wait_recv()
                    theirs = slot[ACROSS]
                    for i in range(1, GROUP):
                        theirs = theirs + slot[ACROSS + i]
                    slot[OTHER] = theirs

            mine, theirs = slot[HALF], slot[OTHER]
            packed = jnp.concatenate(
                [jnp.where(c == 0, mine, theirs), jnp.where(c == 0, theirs, mine)], axis=0
            )
            return jnp.concatenate([packed[:, :n], packed[:, n:]], axis=0) * (1.0 / total)

        return begin, spread, collect, end, further

    gram_begin, gram_spread, gram_collect, gram_end, gram_used = reduction(0)
    proj_begin, proj_spread, proj_collect, proj_end, proj_used = reduction(1)

    greet(ready.at[0], r > 0, -1)
    greet(ready.at[0], lower_two, -2)
    every = jnp.concatenate([tiles_ref[t] for t in range(12)], axis=1)
    gram_begin(inner(every))

    lane = lax.broadcasted_iota(jnp.int32, (n, 128), 1)

    def forward(values):
        return jnp.where(lane == 127, 0.0, pltpu.roll(values, 127, 1)) - values

    def backward(values):
        return values - jnp.where(lane == 0, 0.0, pltpu.roll(values, 1, 1))

    def ex(y):
        return tiles_ref[3 * y] if y < 4 else beside[0]

    def ey(y):
        return tiles_ref[3 * y + 1]

    def ez(y):
        return tiles_ref[3 * y + 2] if y < 4 else beside[2]

    def combine(y):
        up_out[y, pl.ds(0, n)] = ey(y) + (ex(y + 1) - ex(y))
        up_out[y, pl.ds(n, n)] = ez(y) + forward(ex(y))

    up_out[0, pl.ds(2 * n, 4)] = mu
    for y in range(3):
        combine(y)

    @pl.when(r < peers - 1)
    def _():
        pl.semaphore_wait(ready.at[0], count(r < peers - 1, upper_two))

    greet(ready.at[1], lower_two, -2)
    greet(ready.at[1], upper_two, 2)

    @pl.when(lower_two | upper_two)
    def _():
        pl.semaphore_wait(ready.at[1], count(lower_two, upper_two))

    if size > 4:
        pl.semaphore_signal(ready.at[2], inc=1, device_id=other(4), device_id_type=MESH)
        pl.semaphore_wait(ready.at[2], 1)
    gram_spread()

    @pl.when(c == 0)
    def _():
        beside_copy.wait_recv()

    combine(3)

    odd = lax.rem(r, 2) == 1

    @pl.when(jnp.logical_not(odd) & (r < peers - 1))
    def _():
        for copy in up[:2]:
            copy.start()

    curl_x = [ez(y + 1) - ez(y) - forward(ey(y)) for y in range(4)]
    m_x = [mu_y[y] * curl_x[y] for y in range(4)]
    left = jnp.concatenate(
        m_x + [-eps_y[y] * tiles_ref[3 * y + comp] for y in range(4) for comp in range(3)], axis=1
    )
    right = jnp.concatenate(curl_x + [tiles_ref[t] for y in range(4) for t in range(3 * y, 3 * y + 3)], axis=1)
    partial = inner(left, right)
    edge_out[0] = m_x[3]

    curl_y, curl_z, m_y, m_z = [], [], [], []
    for y in range(4):

        @pl.when(r < peers - 1)
        def _():
            down[y].wait_recv()

        if y == 3:

            @pl.when(odd)
            def _():
                sent_all(BELOW, below)

            @pl.when(odd & (r < peers - 1))
            def _():
                for copy in up[:2]:
                    copy.start()


            @pl.when(r < peers - 1)
            def _():
                down[4].wait_recv()

        curl_y.append(up_out[y, pl.ds(n, n)] - below[2 * y + 1])
        curl_z.append(below[2 * y] - up_out[y, pl.ds(0, n)])
        m_y.append(mu_y[y] * curl_y[y])
        m_z.append(mu_y[y] * curl_z[y])
        partial = partial + inner(
            jnp.concatenate([m_y[y], m_z[y]], axis=1), jnp.concatenate([curl_y[y], curl_z[y]], axis=1)
        )
    proj_begin(partial)
    edge_out[1] = m_z[3]

    @pl.when(c == 0)
    def _():
        edge_copy.start()

    proj_spread()

    @pl.when(r < peers - 1)
    def _():
        for copy in up[2:]:
            copy.start()

    gram_collect()
    gram_matrix = gram_end()
    wide = factor(gram_matrix)
    upper_ref[...] = wide[:, :n]
    inverse = wide[:, n:]
    left = left_terms(inverse)

    def put(target, y, comp, value):
        target[pl.ds(comp * 4 + y, n, stride=12), :] = times(left, value)

    for place in range(12):
        put(ortho_ref, place // 3, place % 3, tiles_ref[place])

    @pl.when(c == 1)
    def _():
        edge_copy.wait_recv()

    def finish_x():
        before_z = [edge[1]] + m_z[:3]
        for y in range(4):
            image_x = (m_z[y] - before_z[y]) - backward(m_y[y]) - eps_y[y] * ex(y)
            put(applied_ref, y, 0, image_x)

    def finish_yz(y):
        before_x = edge[0] if y == 0 else m_x[y - 1]
        lower_mu = over(up_in[0, pl.ds(2 * n + y, 1)])
        lower_z = lower_mu * (ey(y) - up_in[y, pl.ds(0, n)])
        lower_y = lower_mu * (up_in[y, pl.ds(n, n)] - ez(y))
        image_y = backward(m_x[y]) - (m_z[y] - lower_z) - eps_y[y] * ey(y)
        image_z = (m_y[y] - lower_y) - (m_x[y] - before_x) - eps_y[y] * ez(y)
        put(applied_ref, y, 1, image_y)
        put(applied_ref, y, 2, image_z)


    @pl.when(first)
    def _():
        finish_x()
        for y in range(4):
            finish_yz(y)

    proj_collect()

    @pl.when(r > 0)
    def _():
        for copy in up[:3]:
            copy.wait_recv()
        finish_x()
        for y in range(3):
            finish_yz(y)

    half = times(left, proj_end())
    projected_ref[...] = inner(half, inverse)

    @pl.when(r > 0)
    def _():
        up[3].wait_recv()
        finish_yz(3)

    for copy in gram_used + proj_used:
        copy.wait_send()
    rows_sent = 2 * (len(near) + 2) * (n // 4)
    if single:

        @pl.when(first)
        def _():
            sent_all(SUMS, landed.at[pl.ds(0, rows_sent)])

        @pl.when(r > 0)
        def _():
            sent_all(SUMS, landed.at[pl.ds(0, rows_sent + n // 4)])

    else:
        sent_all(SUMS, landed.at[pl.ds(0, rows_sent)])

    @pl.when(c == 1)
    def _():
        beside_copy.wait_send()

    @pl.when(c == 0)
    def _():
        edge_copy.wait_send()

    @pl.when((r > 0) & jnp.logical_not(odd))
    def _():
        sent_all(BELOW, below)

    @pl.when(r < peers - 1)
    def _():
        sent_all(ABOVE, landed.at[pl.ds(0, 8 * n + 8)])


def last_kernel(*refs):
    sources, targets, semaphores = refs[:4], refs[4:8], refs[8]
    copies = [
        pltpu.make_async_copy(source, target, semaphores.at[i])
        for i, (source, target) in enumerate(zip(sources, targets))
    ]
    for copy in copies:
        copy.start()
    for copy in copies:
        copy.wait()


def local(peers, columns_of, krylov_basis, regions, mu_table, eps_table, shift_value):
    n = krylov_basis.shape[0]
    flat = krylov_basis.reshape(n * 12, 128)
    total = 3 * peers * columns_of * 4 * 128
    more = max(peers.bit_length() - 4, 0)
    received = REDUCE + 2 * (4 + more)
    sent = FURTHER + 2 * more
    tile = (n, 128)
    vmem = pl.BlockSpec(memory_space=pltpu.VMEM)
    shapes = [
        jax.ShapeDtypeStruct((n * 12, 128), F32),
        jax.ShapeDtypeStruct((n, n), F32),
        jax.ShapeDtypeStruct((n * 12, 128), F32),
        jax.ShapeDtypeStruct((n, n), F32),
    ]
    results = pl.pallas_call(
        functools.partial(main_kernel, peers, total),
        out_shape=shapes,
        in_specs=[pl.BlockSpec(memory_space=pltpu.HBM)] * 5,
        out_specs=[vmem] * 4,
        scratch_shapes=[
            pltpu.VMEM((12,) + tile, F32),
            pltpu.VMEM((n * 12, 128), F32),
            pltpu.VMEM((8,) + tile, F32),
            pltpu.VMEM((3,) + tile, F32),
            pltpu.VMEM((2,) + tile, F32),
            pltpu.VMEM((2,) + tile, F32),
            pltpu.VMEM((4, 2 * n + 8, 128), F32),
            pltpu.VMEM((4, 2 * n + 8, 128), F32),
            pltpu.VMEM((2, MORE + 2 * more, n // 4, 2 * n), F32),
            pltpu.VMEM(regions.shape, regions.dtype),
            pltpu.VMEM(mu_table.shape, F32),
            pltpu.VMEM(eps_table.shape, F32),
            pltpu.VMEM(shift_value.shape, F32),
            pltpu.SemaphoreType.DMA((5,)),
            pltpu.SemaphoreType.DMA((sent,)),
            pltpu.SemaphoreType.DMA((received,)),
            pltpu.SemaphoreType.REGULAR((3,)),
        ],
        compiler_params=pltpu.CompilerParams(collective_id=0, has_side_effects=True, vmem_limit_bytes=32 << 20),
        name="gather_and_factor",
    )(
        *(pltpu.with_memory_space_constraint(array, pltpu.HBM) for array in (flat, regions, mu_table, eps_table)),
        shift_value,
    )
    ortho, upper, applied, projected = pl.pallas_call(
        last_kernel,
        out_shape=shapes,
        in_specs=[vmem] * 4,
        out_specs=[pl.BlockSpec(memory_space=pl.ANY)] * 4,
        scratch_shapes=[pltpu.SemaphoreType.DMA((4,))],
        compiler_params=pltpu.CompilerParams(vmem_limit_bytes=16 << 20),
        name="hand_over",
    )(*results)
    return ortho.reshape(krylov_basis.shape), upper, applied.reshape(krylov_basis.shape), projected


def solution(mesh):
    peers = mesh.shape["row"]
    columns_of = mesh.shape["col"] * 1
    placed = (P("shift", None, "row", "col", None), P("row", "col", None), P(), P(), P("shift"))
    return jax.shard_map(
        functools.partial(local, peers, columns_of),
        mesh=mesh,
        in_specs=placed,
        out_specs=(
            P("shift", None, "row", "col", None),
            P("shift", None),
            P("shift", None, "row", "col", None),
            P("shift", None),
        ),
        check_vma=False,
    )
```

```python
import functools

import jax
import jax.numpy as jnp
from jax import lax
from jax.experimental import pallas as pl
from jax.experimental.pallas import tpu as pltpu
from jax.sharding import PartitionSpec as P

F32 = jnp.float32
BF16 = jnp.bfloat16
MESH = pl.DeviceIdType.MESH
SIDE, DOWN, UP = 0, 1, 6
REDUCE = 10
BELOW, ABOVE, SUMS, FURTHER = 1, 2, 3, 4
GROUP = 8
PAIR_OUT, PAIR_IN, HALF, OTHER, MINE, OTHERS = 0, 1, 2, 3, 4, 5
ACROSS = OTHERS + GROUP - 1
MORE = ACROSS + GROUP


def split3(x):
    high = x.astype(BF16)
    rest = x - high.astype(F32)
    mid = rest.astype(BF16)
    low = (rest - mid.astype(F32)).astype(BF16)
    return high, mid, low


def rows_dot(a, b):
    return lax.dot_general(a, b, (((1,), (1,)), ((), ())), preferred_element_type=F32)


def plain_dot(a, b):
    return lax.dot_general(a, b, (((1,), (0,)), ((), ())), preferred_element_type=F32)


def first_dot(a, b):
    return lax.dot_general(a, b, (((0,), (0,)), ((), ())), preferred_element_type=F32)


def inner(left, right=None):
    n = left.shape[0]
    a, b, c = split3(left)
    d, e, f = (a, b, c) if right is None else split3(right)
    first = rows_dot(jnp.concatenate([a, b, c], axis=0), d)
    second = rows_dot(jnp.concatenate([a, b], axis=0), e)
    third = rows_dot(a, f)
    return first[:n] + ((first[n : 2 * n] + second[:n]) + ((first[2 * n :] + third) + second[n:]))


def left_terms(left):
    a, b, c = split3(left)
    return jnp.concatenate([a, a, b, b, a, c], axis=1)


def times(left, right):
    d, e, f = split3(right)
    return plain_dot(left, jnp.concatenate([d, e, d, e, f, d], axis=0))


def factor(gram):
    n = gram.shape[0]
    size = 16
    wide = 2 * n
    rows_of = lax.broadcasted_iota(jnp.int32, (n, n), 0)
    eye = (rows_of == lax.broadcasted_iota(jnp.int32, (n, n), 1)).astype(F32)
    rest = jnp.concatenate([gram, eye], axis=1)
    place = lax.broadcasted_iota(jnp.int32, (size, wide), 0)
    done, pivots = [], []
    for block in range(n // size):
        rows = rest[:size]
        begin = block * size
        cols = [
            jnp.broadcast_to(rows[:, begin + j : begin + j + 1], (size, wide)) for j in range(size)
        ]
        pivot = jnp.zeros((size, wide), F32)
        inverse = jnp.zeros((size, wide), F32)
        for k in range(size):
            head = jnp.broadcast_to(cols[k][k : k + 1], (size, wide))
            reciprocal = 1.0 / head
            pivot = jnp.where(place == k, head, pivot)
            inverse = jnp.where(place == k, reciprocal, inverse)
            if k < size - 1:
                ratio = jnp.where(place > k, cols[k] * reciprocal, 0.0)
                for j in range(k + 1, size):
                    cols[j] = cols[j] - ratio * jnp.broadcast_to(cols[j][k : k + 1], (size, wide))
                rows = rows - ratio * jnp.broadcast_to(rows[k : k + 1], (size, wide))
        done.append(rows)
        pivots.append(pivot)
        if begin + size < n:
            a, b, c = split3((rows * inverse)[:, :n])
            d, e, f = split3(rows)
            update = first_dot(
                jnp.concatenate([a, a, b, b, a, c], axis=0),
                jnp.concatenate([d, e, d, e, f, d], axis=0),
            )
            rest = rest[size:] - update[begin + size :]
    pivot = jnp.concatenate(pivots, axis=0)
    scaled = jnp.concatenate(done, axis=0) / jnp.sqrt(pivot)
    keep = lax.broadcasted_iota(jnp.int32, (n, wide), 1) >= lax.broadcasted_iota(
        jnp.int32, (n, wide), 0
    )
    return jnp.where(keep, scaled, 0.0)


def main_kernel(
    peers,
    total,
    x_ref,
    regions_ref,
    mu_ref,
    eps_ref,
    shift_ref,
    ortho_ref,
    upper_ref,
    applied_ref,
    projected_ref,
    tiles_ref,
    landed,
    below,
    beside,
    edge,
    edge_out,
    up_out,
    up_in,
    sums,
    labels_ref,
    mu_table_ref,
    eps_table_ref,
    shift_table_ref,
    load_sem,
    send_sem,
    recv_sem,
    ready,
):
    r = lax.axis_index("row")
    c = lax.axis_index("col")
    n = landed.shape[0] // 12
    first, last = r == 0, r == peers - 1
    bits = peers.bit_length() - 1
    near = [m for m in range(1, GROUP) if m < peers]
    more = [m for m in (1 << b for b in range(bits)) if m >= GROUP]
    inside = lax.rem(r, GROUP)
    single = peers == GROUP
    exchange = jnp.logical_not(first) if single else r >= 0

    def other(mask):
        return {"row": jnp.bitwise_xor(r, mask)}

    sibling = {"col": 1 - c}
    load = pltpu.make_async_copy(x_ref, landed, load_sem.at[0])
    load.start()

    size = min(GROUP, peers)
    lower_two, upper_two = inside >= 2, inside < size - 2
    barrier = pltpu.get_barrier_semaphore()

    def greet(semaphore, condition, step):
        @pl.when(condition)
        def _():
            pl.semaphore_signal(semaphore, inc=1, device_id={"row": r + step}, device_id_type=MESH)

    def count(*conditions):
        return sum(jnp.where(condition, 1, 0) for condition in conditions)

    pl.semaphore_signal(barrier, inc=1, device_id=sibling, device_id_type=MESH)
    for mask in more:
        pl.semaphore_signal(barrier, inc=1, device_id=other(mask), device_id_type=MESH)
    greet(barrier, r < peers - 1, 1)
    greet(barrier, upper_two, 2)

    small = [
        pltpu.make_async_copy(regions_ref, labels_ref, load_sem.at[1]),
        pltpu.make_async_copy(mu_ref, mu_table_ref, load_sem.at[2]),
        pltpu.make_async_copy(eps_ref, eps_table_ref, load_sem.at[3]),
        pltpu.make_async_copy(shift_ref, shift_table_ref, load_sem.at[4]),
    ]
    for copy in small:
        copy.start()

    load.wait()
    for y in range(4):
        for comp in range(3):
            tiles_ref[3 * y + comp] = landed[pl.ds(comp * 4 + y, n, stride=12), :]

    def remote(sent, index, source, target, device):
        return pltpu.make_async_remote_copy(
            src_ref=source,
            dst_ref=target,
            send_sem=send_sem.at[sent],
            recv_sem=recv_sem.at[index],
            device_id=device,
            device_id_type=MESH,
        )

    def sent_all(sent, like):
        remote(sent, 0, like, like, sibling).wait_send()

    beside_copy = remote(SIDE, SIDE, tiles_ref.at[pl.ds(0, 3)], beside, sibling)
    edge_copy = remote(SIDE, SIDE, edge_out, edge, sibling)
    lower = {"row": jnp.maximum(r - 1, 0)}
    upper = {"row": jnp.minimum(r + 1, peers - 1)}
    down = [
        remote(BELOW, DOWN + i, tiles_ref.at[pl.ds(3 * y + 1 + k, m)], below.at[pl.ds(2 * y + k, m)], lower)
        for i, (y, k, m) in enumerate([(0, 0, 2), (1, 0, 2), (2, 0, 2), (3, 0, 1), (3, 1, 1)])
    ]
    up = []
    for y in range(4):
        part = pl.ds(0, 2 * n + 8 if y == 0 else 2 * n)
        up.append(remote(ABOVE, UP + y, up_out.at[y, part], up_in.at[y, part], upper))

    @pl.when(last)
    def _():
        below[...] = jnp.zeros_like(below)

    @pl.when(first)
    def _():
        up_in[...] = jnp.zeros_like(up_in)

    @pl.when(c == 1)
    def _():
        beside[...] = jnp.zeros_like(beside)

    @pl.when(c == 0)
    def _():
        edge[...] = jnp.zeros_like(edge)

    pl.semaphore_wait(barrier, 1 + len(more) + count(r > 0, lower_two))
    @pl.when(c == 1)
    def _():
        beside_copy.start()

    @pl.when(r > 0)
    def _():
        for copy in down:
            copy.start()

    for copy in small:
        copy.wait()
    labels = labels_ref[0]

    def entry(table, region):
        return jnp.broadcast_to(table[...][None, region : region + 1], labels.shape)

    mu = jnp.zeros(labels.shape, F32)
    eps = jnp.zeros(labels.shape, F32)
    for region in range(mu_table_ref.shape[0]):
        mu = jnp.where(labels == region, entry(mu_table_ref, region), mu)
        eps = jnp.where(labels == region, entry(eps_table_ref, region), eps)
    eps = eps * entry(shift_table_ref, 0)

    def over(row):
        return jnp.broadcast_to(row, (n, 128))

    mu_y = [over(mu[y : y + 1]) for y in range(4)]
    eps_y = [over(eps[y : y + 1]) for y in range(4)]

    def reduction(which):
        base = REDUCE + which * (4 + len(more))
        slot = sums.at[which]
        both = single and which == 1
        swap = exchange if both else r >= 0
        pair = remote(SUMS, base, slot.at[PAIR_OUT], slot.at[PAIR_IN], sibling)
        back = remote(SUMS, base + 1, slot.at[HALF], slot.at[OTHER], sibling)
        direct = [
            remote(SUMS, base + 2, slot.at[MINE], slot.at[OTHERS + mask - 1], other(mask))
            for mask in near
        ]
        everyone = slot.at[pl.ds(OTHERS, len(near))]
        arrived = remote(SUMS, base + 2, everyone, everyone, sibling)
        further = [
            remote(
                FURTHER + which * len(more) + i,
                base + 4 + i,
                slot.at[MORE + 2 * i],
                slot.at[MORE + 2 * i + 1],
                other(mask),
            )
            for i, mask in enumerate(more)
        ]

        across = both and remote(
            SUMS,
            base + 3,
            slot.at[MINE],
            slot.at[ACROSS + lax.rem(r + GROUP - 1, GROUP)],
            {"row": 0, "col": 1 - c},
        )
        everything = slot.at[pl.ds(ACROSS, GROUP)]
        gathered = both and remote(SUMS, base + 3, everything, everything, sibling)

        def begin(value):
            packed = jnp.concatenate([value[: n // 2], value[n // 2 :]], axis=1)
            q = n // 4
            slot[PAIR_OUT] = jnp.where(c == 0, packed[q:], packed[:q])
            slot[MINE] = jnp.where(c == 0, packed[:q], packed[q:])
            pair.start()

        def spread():
            pair.wait_recv()
            slot[MINE] = slot[MINE] + slot[PAIR_IN]
            if both:
                across.start()
            for copy in reversed(direct):
                copy.start()

        def collect():
            got = slot[MINE]
            arrived.wait_recv()
            for mask in near:
                got = got + slot[OTHERS + mask - 1]
            for i, copy in enumerate(further):
                slot[MORE + 2 * i] = got
                copy.start()
                copy.wait_recv()
                got = got + slot[MORE + 2 * i + 1]
            slot[HALF] = got

            @pl.when(swap)
            def _():
                back.start()

        def end():
            @pl.when(swap)
            def _():
                back.wait_recv()

            if both:

                @pl.when(first)
                def _():
                    gathered.wait_recv()
                    theirs = slot[ACROSS]
                    for i in range(1, GROUP):
                        theirs = theirs + slot[ACROSS + i]
                    slot[OTHER] = theirs

            mine, theirs = slot[HALF], slot[OTHER]
            packed = jnp.concatenate(
                [jnp.where(c == 0, mine, theirs), jnp.where(c == 0, theirs, mine)], axis=0
            )
            return jnp.concatenate([packed[:, :n], packed[:, n:]], axis=0) * (1.0 / total)

        return begin, spread, collect, end, further

    gram_begin, gram_spread, gram_collect, gram_end, gram_used = reduction(0)
    proj_begin, proj_spread, proj_collect, proj_end, proj_used = reduction(1)

    greet(ready.at[0], r > 0, -1)
    greet(ready.at[0], lower_two, -2)
    every = jnp.concatenate([tiles_ref[t] for t in range(12)], axis=1)
    gram_begin(inner(every))

    lane = lax.broadcasted_iota(jnp.int32, (n, 128), 1)

    def forward(values):
        return jnp.where(lane == 127, 0.0, pltpu.roll(values, 127, 1)) - values

    def backward(values):
        return values - jnp.where(lane == 0, 0.0, pltpu.roll(values, 1, 1))

    def ex(y):
        return tiles_ref[3 * y] if y < 4 else beside[0]

    def ey(y):
        return tiles_ref[3 * y + 1]

    def ez(y):
        return tiles_ref[3 * y + 2] if y < 4 else beside[2]

    def combine(y):
        up_out[y, pl.ds(0, n)] = ey(y) + (ex(y + 1) - ex(y))
        up_out[y, pl.ds(n, n)] = ez(y) + forward(ex(y))

    up_out[0, pl.ds(2 * n, 4)] = mu
    for y in range(3):
        combine(y)

    @pl.when(r < peers - 1)
    def _():
        pl.semaphore_wait(ready.at[0], count(r < peers - 1, upper_two))

    greet(ready.at[1], lower_two, -2)
    greet(ready.at[1], upper_two, 2)

    @pl.when(lower_two | upper_two)
    def _():
        pl.semaphore_wait(ready.at[1], count(lower_two, upper_two))

    if size > 4:
        pl.semaphore_signal(ready.at[2], inc=1, device_id=other(4), device_id_type=MESH)
        pl.semaphore_wait(ready.at[2], 1)
    gram_spread()

    @pl.when(c == 0)
    def _():
        beside_copy.wait_recv()

    combine(3)

    odd = lax.rem(r, 2) == 1

    @pl.when(jnp.logical_not(odd) & (r < peers - 1))
    def _():
        for copy in up[:2]:
            copy.start()

    curl_x = [ez(y + 1) - ez(y) - forward(ey(y)) for y in range(4)]
    m_x = [mu_y[y] * curl_x[y] for y in range(4)]
    left = jnp.concatenate(
        m_x + [-eps_y[y] * tiles_ref[3 * y + comp] for y in range(4) for comp in range(3)], axis=1
    )
    right = jnp.concatenate(curl_x + [tiles_ref[t] for y in range(4) for t in range(3 * y, 3 * y + 3)], axis=1)
    partial = inner(left, right)
    edge_out[0] = m_x[3]

    curl_y, curl_z, m_y, m_z = [], [], [], []
    for y in range(4):

        if y == 3:

            @pl.when(odd & (c == 0))
            def _():
                sent_all(BELOW, below)

            @pl.when(odd & (c == 0) & (r < peers - 1))
            def _():
                for copy in up[:2]:
                    copy.start()

        @pl.when(r < peers - 1)
        def _():
            down[y].wait_recv()

        if y == 3:

            @pl.when(odd & (c == 1))
            def _():
                sent_all(BELOW, below)

            @pl.when(odd & (c == 1) & (r < peers - 1))
            def _():
                for copy in up[:2]:
                    copy.start()

            @pl.when(r < peers - 1)
            def _():
                down[4].wait_recv()

        curl_y.append(up_out[y, pl.ds(n, n)] - below[2 * y + 1])
        curl_z.append(below[2 * y] - up_out[y, pl.ds(0, n)])
        m_y.append(mu_y[y] * curl_y[y])
        m_z.append(mu_y[y] * curl_z[y])
        partial = partial + inner(
            jnp.concatenate([m_y[y], m_z[y]], axis=1), jnp.concatenate([curl_y[y], curl_z[y]], axis=1)
        )
    proj_begin(partial)
    edge_out[1] = m_z[3]

    @pl.when(c == 0)
    def _():
        edge_copy.start()

    proj_spread()

    @pl.when(jnp.logical_not(odd) & (r < peers - 1))
    def _():
        for copy in up[2:]:
            copy.start()

    gram_collect()

    @pl.when(odd & (r < peers - 1))
    def _():
        for copy in up[2:]:
            copy.start()
    gram_matrix = gram_end()
    wide = factor(gram_matrix)
    upper_ref[...] = wide[:, :n]
    inverse = wide[:, n:]
    left = left_terms(inverse)

    def put(target, y, comp, value):
        target[pl.ds(comp * 4 + y, n, stride=12), :] = times(left, value)

    for place in range(12):
        put(ortho_ref, place // 3, place % 3, tiles_ref[place])

    @pl.when(c == 1)
    def _():
        edge_copy.wait_recv()

    def finish_x():
        before_z = [edge[1]] + m_z[:3]
        for y in range(4):
            image_x = (m_z[y] - before_z[y]) - backward(m_y[y]) - eps_y[y] * ex(y)
            put(applied_ref, y, 0, image_x)

    def finish_yz(y):
        before_x = edge[0] if y == 0 else m_x[y - 1]
        lower_mu = over(up_in[0, pl.ds(2 * n + y, 1)])
        lower_z = lower_mu * (ey(y) - up_in[y, pl.ds(0, n)])
        lower_y = lower_mu * (up_in[y, pl.ds(n, n)] - ez(y))
        image_y = backward(m_x[y]) - (m_z[y] - lower_z) - eps_y[y] * ey(y)
        image_z = (m_y[y] - lower_y) - (m_x[y] - before_x) - eps_y[y] * ez(y)
        put(applied_ref, y, 1, image_y)
        put(applied_ref, y, 2, image_z)


    @pl.when(first)
    def _():
        finish_x()
        for y in range(4):
            finish_yz(y)

    proj_collect()

    @pl.when(r > 0)
    def _():
        for copy in up[:3]:
            copy.wait_recv()
        finish_x()
        for y in range(3):
            finish_yz(y)

    half = times(left, proj_end())
    projected_ref[...] = inner(half, inverse)

    @pl.when(r > 0)
    def _():
        up[3].wait_recv()
        finish_yz(3)

    for copy in gram_used + proj_used:
        copy.wait_send()
    rows_sent = 2 * (len(near) + 2) * (n // 4)
    if single:

        @pl.when(first)
        def _():
            sent_all(SUMS, landed.at[pl.ds(0, rows_sent)])

        @pl.when(r > 0)
        def _():
            sent_all(SUMS, landed.at[pl.ds(0, rows_sent + n // 4)])

    else:
        sent_all(SUMS, landed.at[pl.ds(0, rows_sent)])

    @pl.when(c == 1)
    def _():
        beside_copy.wait_send()

    @pl.when(c == 0)
    def _():
        edge_copy.wait_send()

    @pl.when((r > 0) & jnp.logical_not(odd))
    def _():
        sent_all(BELOW, below)

    @pl.when(r < peers - 1)
    def _():
        sent_all(ABOVE, landed.at[pl.ds(0, 8 * n + 8)])


def last_kernel(*refs):
    sources, targets, semaphores = refs[:4], refs[4:8], refs[8]
    copies = [
        pltpu.make_async_copy(source, target, semaphores.at[i])
        for i, (source, target) in enumerate(zip(sources, targets))
    ]
    for copy in copies:
        copy.start()
    for copy in copies:
        copy.wait()


def local(peers, columns_of, krylov_basis, regions, mu_table, eps_table, shift_value):
    n = krylov_basis.shape[0]
    flat = krylov_basis.reshape(n * 12, 128)
    total = 3 * peers * columns_of * 4 * 128
    more = max(peers.bit_length() - 4, 0)
    received = REDUCE + 2 * (4 + more)
    sent = FURTHER + 2 * more
    tile = (n, 128)
    vmem = pl.BlockSpec(memory_space=pltpu.VMEM)
    shapes = [
        jax.ShapeDtypeStruct((n * 12, 128), F32),
        jax.ShapeDtypeStruct((n, n), F32),
        jax.ShapeDtypeStruct((n * 12, 128), F32),
        jax.ShapeDtypeStruct((n, n), F32),
    ]
    results = pl.pallas_call(
        functools.partial(main_kernel, peers, total),
        out_shape=shapes,
        in_specs=[pl.BlockSpec(memory_space=pltpu.HBM)] * 5,
        out_specs=[vmem] * 4,
        scratch_shapes=[
            pltpu.VMEM((12,) + tile, F32),
            pltpu.VMEM((n * 12, 128), F32),
            pltpu.VMEM((8,) + tile, F32),
            pltpu.VMEM((3,) + tile, F32),
            pltpu.VMEM((2,) + tile, F32),
            pltpu.VMEM((2,) + tile, F32),
            pltpu.VMEM((4, 2 * n + 8, 128), F32),
            pltpu.VMEM((4, 2 * n + 8, 128), F32),
            pltpu.VMEM((2, MORE + 2 * more, n // 4, 2 * n), F32),
            pltpu.VMEM(regions.shape, regions.dtype),
            pltpu.VMEM(mu_table.shape, F32),
            pltpu.VMEM(eps_table.shape, F32),
            pltpu.VMEM(shift_value.shape, F32),
            pltpu.SemaphoreType.DMA((5,)),
            pltpu.SemaphoreType.DMA((sent,)),
            pltpu.SemaphoreType.DMA((received,)),
            pltpu.SemaphoreType.REGULAR((3,)),
        ],
        compiler_params=pltpu.CompilerParams(collective_id=0, has_side_effects=True, vmem_limit_bytes=32 << 20),
        name="gather_and_factor",
    )(
        *(pltpu.with_memory_space_constraint(array, pltpu.HBM) for array in (flat, regions, mu_table, eps_table)),
        shift_value,
    )
    ortho, upper, applied, projected = pl.pallas_call(
        last_kernel,
        out_shape=shapes,
        in_specs=[vmem] * 4,
        out_specs=[pl.BlockSpec(memory_space=pl.ANY)] * 4,
        scratch_shapes=[pltpu.SemaphoreType.DMA((4,))],
        compiler_params=pltpu.CompilerParams(vmem_limit_bytes=16 << 20),
        name="hand_over",
    )(*results)
    return ortho.reshape(krylov_basis.shape), upper, applied.reshape(krylov_basis.shape), projected


def solution(mesh):
    peers = mesh.shape["row"]
    columns_of = mesh.shape["col"] * 1
    placed = (P("shift", None, "row", "col", None), P("row", "col", None), P(), P(), P("shift"))
    return jax.shard_map(
        functools.partial(local, peers, columns_of),
        mesh=mesh,
        in_specs=placed,
        out_specs=(
            P("shift", None, "row", "col", None),
            P("shift", None),
            P("shift", None, "row", "col", None),
            P("shift", None),
        ),
        check_vma=False,
    )
```
